32 devices in a mesh: vid: 4 (over z), aud: 8 (over y, x, core).
Axes of the slice: x: 2, y: 2, z: 4, core: 2. Of those that a mesh axis runs over, the one named last changes fastest.
Arguments:
- video_tokens: bfloat16 [4096, 4096], P(('vid', 'aud')), may hold values from -28 to 28
- audio_tokens: bfloat16 [4096, 4096], P(('aud', 'vid')), may hold values from -28 to 28
- pair_weight: bfloat16 [4096, 256], replicated, may hold values from -0.125 to 0.125
- video_value: bfloat16 [4096, 256], replicated, may hold values from -0.125 to 0.125
- audio_value: bfloat16 [4096, 256], replicated, may hold values from -0.125 to 0.125
- video_output: bfloat16 [256, 4096], replicated, may hold values from -1 to 1
- audio_output: bfloat16 [256, 4096], replicated, may hold values from -1 to 1
- video_cotangent: bfloat16 [4096, 4096], P(('vid', 'aud')), may hold values from -0.59765625 to 0.59765625
- audio_cotangent: bfloat16 [4096, 4096], P(('aud', 'vid')), may hold values from -0.59765625 to 0.59765625
Outputs:
- video_result: bfloat16 [4096, 4096], P(('vid', 'aud'))
- audio_result: bfloat16 [4096, 4096], P(('aud', 'vid'))
- video_gradient: bfloat16 [4096, 4096], P(('vid', 'aud'))
- audio_gradient: bfloat16 [4096, 4096], P(('aud', 'vid'))
The draws below stay inside these ranges and needn't reach their ends.
All inputs are finite; a program needn't handle non-finite values.
Results may differ from the reference program's by a relative error of at most 0.015.
The reference program's roundings to bfloat16 on the way (of `score_grad`) count: a program that leaves them out, or rounds other values in their place, can miss the bound.
Values may be sent and summed in bfloat16 or wider, within the bound.
A program may use at most 192 MiB of HBM per device.

```python
import jax
import jax.numpy as jnp
from jax import lax

D = 4096
HS = 128
HEADS = 2
TV = 128
TA = 128
HD = 256
NV = 4096
NA = 4096
N_VID = 4
N_AUD = 8


def shared_rows(key):
    base_key = jax.random.fold_in(key, 11)
    key_video, key_audio = jax.random.split(base_key, 2)
    video_rows = jnp.clip(jax.random.normal(key_video, (NV, D), jnp.float32), -6.0, 6.0)
    audio_rows = jnp.clip(jax.random.normal(key_audio, (NA, D), jnp.float32), -6.0, 6.0)
    return (video_rows, audio_rows)


def draw_video_tokens(key, part):
    return shared_rows(key)[0].astype(jnp.bfloat16)


def draw_audio_tokens(key, part):
    return shared_rows(key)[1].astype(jnp.bfloat16)


def block_scale(own_key, extent, pieces, least, high):
    gain, own = 1.0, jax.random.fold_in(own_key, 6)
    for position, parts in pieces:
        draws = jnp.exp(jax.random.uniform(jax.random.fold_in(own, position), (parts,), jnp.float32, least / len(pieces), high / len(pieces)))
        gain = gain * jnp.repeat(draws, extent[position] // parts).reshape([-1 if axis == position else 1 for axis in range(len(extent))])
    return gain


def scatter_about(stream_key, dims, scale, limit, cuts=(), kind=jnp.bfloat16):
    level = block_scale(stream_key, dims, cuts, -0.22, 0.18) if cuts else 1.0
    drawn = jax.random.normal(stream_key, dims, jnp.float32) * scale * level
    return jnp.minimum(jnp.maximum(drawn, -limit), limit).astype(kind)


def setup_inputs(seed: int = 0) -> dict:
    arg_keys = jax.random.split(jax.random.key(seed), 10)
    video_tokens = draw_video_tokens(jax.random.fold_in(arg_keys[9], 71), 0)
    audio_tokens = draw_audio_tokens(jax.random.fold_in(arg_keys[9], 71), 0)
    pair_weight = scatter_about(arg_keys[2], (D, HD), (D // 2) ** -0.5, 0.125)
    video_value = scatter_about(arg_keys[3], (D, HD), (D // 2) ** -0.5, 0.125)
    audio_value = scatter_about(arg_keys[4], (D, HD), (D // 2) ** -0.5, 0.125)
    video_output = scatter_about(arg_keys[5], (HD, D), 0.2, 1.0)
    audio_output = scatter_about(arg_keys[6], (HD, D), 0.2, 1.0)
    video_cotangent = scatter_about(arg_keys[7], (NV, D), 0.1, 0.59765625, ((0, 32),))
    audio_cotangent = scatter_about(arg_keys[8], (NA, D), 0.1, 0.59765625, ((0, 32),))
    return {"video_tokens": video_tokens, "audio_tokens": audio_tokens, "pair_weight": pair_weight, "video_value": video_value, "audio_value": audio_value, "video_output": video_output, "audio_output": audio_output, "video_cotangent": video_cotangent, "audio_cotangent": audio_cotangent}


def tile_scores(left_rows, right_rows, score_scale):
    return score_scale * lax.dot_general(left_rows, right_rows, (((1,), (1,)), ((), ())), preferred_element_type=jnp.float32)


def rounded(values):
    return lax.optimization_barrier(values.astype(jnp.bfloat16)).astype(jnp.float32)


def blockwise(weights, right_rows, blocks, block_size, factor):
    left_part = weights.astype(jnp.float32).reshape(weights.shape[0], blocks, block_size)
    right_part = right_rows.astype(jnp.float32).reshape(blocks, block_size, right_rows.shape[1])
    partials = factor * jnp.einsum("vjk,jkh->jvh", left_part, right_part)
    return jnp.sum(rounded(partials), axis=0)


def transposed(weights, right_rows, factor):
    return rounded(factor * lax.dot_general(weights, right_rows, (((0,), (0,)), ((), ())), preferred_element_type=jnp.float32))


def reference(video_tokens, audio_tokens, pair_weight, video_value, audio_value, video_output, audio_output, video_cotangent, audio_cotangent):
    bf_type = jnp.bfloat16
    score_scale = float(HS) ** -0.5
    video_block = TV * N_AUD
    audio_block = TA * N_VID
    video_pairs = jnp.dot(video_tokens, pair_weight, preferred_element_type=jnp.float32).astype(bf_type)
    video_values = jnp.dot(video_tokens, video_value, preferred_element_type=jnp.float32).astype(bf_type)
    audio_pairs = jnp.dot(audio_tokens, pair_weight, preferred_element_type=jnp.float32).astype(bf_type)
    audio_values = jnp.dot(audio_tokens, audio_value, preferred_element_type=jnp.float32).astype(bf_type)
    contract_last = (((1,), (1,)), ((), ()))
    video_back = lax.dot_general(video_cotangent, video_output, contract_last, preferred_element_type=jnp.float32).astype(bf_type)
    audio_back = lax.dot_general(audio_cotangent, audio_output, contract_last, preferred_element_type=jnp.float32).astype(bf_type)
    video_mix_heads, audio_mix_heads = [], []
    video_pair_heads, video_value_heads, audio_pair_heads, audio_value_heads = [], [], [], []
    for head_index in range(HEADS):
        offset = head_index * HS
        head_vpairs = video_pairs[:, offset:offset + HS]
        head_apairs = audio_pairs[:, offset:offset + HS]
        head_vvalues = video_values[:, offset:offset + HS]
        head_avalues = audio_values[:, offset:offset + HS]
        head_vback = video_back[:, offset:offset + HS]
        head_aback = audio_back[:, offset:offset + HS]
        col_peak = jnp.full((NA,), -jnp.inf, jnp.float32)
        col_total = jnp.zeros((NA,), jnp.float32)
        for block_index in range(N_VID):
            first_row = block_index * video_block
            scores = tile_scores(head_vpairs[first_row:first_row + video_block], head_apairs, score_scale)
            new_peak = jnp.maximum(col_peak, jnp.max(scores, axis=0))
            col_total = col_total * jnp.exp(col_peak - new_peak) + jnp.sum(jnp.exp(scores - new_peak[None, :]), axis=0)
            col_peak = new_peak

        def probabilities(first_row):
            scores = tile_scores(head_vpairs[first_row:first_row + video_block], head_apairs, score_scale)
            row_exp = jnp.exp(scores - jnp.max(scores, axis=1, keepdims=True))
            row_prob = row_exp / jnp.sum(row_exp, axis=1, keepdims=True)
            col_prob = jnp.exp(scores - col_peak[None, :]) / col_total[None, :]
            return row_prob, col_prob

        video_mix_parts = []
        audio_mix_sum = jnp.zeros((NA, HS), jnp.float32)
        col_delta = jnp.zeros((NA,), jnp.float32)
        for block_index in range(N_VID):
            first_row = block_index * video_block
            row_prob, col_prob = probabilities(first_row)
            row_weight = row_prob.astype(bf_type)
            col_weight = col_prob.astype(bf_type)
            block_vvalues = head_vvalues[first_row:first_row + video_block]
            video_mix_parts.append(blockwise(row_weight, head_avalues, N_AUD, audio_block, 1.0))
            audio_mix_sum = audio_mix_sum + transposed(col_weight, block_vvalues, 1.0)
            col_grad = lax.dot_general(block_vvalues, head_aback, contract_last, preferred_element_type=jnp.float32)
            col_delta = col_delta + jnp.sum(col_prob * col_grad, axis=0)
        video_mix_heads.append(jnp.concatenate(video_mix_parts, axis=0))
        audio_mix_heads.append(audio_mix_sum)
        video_pair_parts, video_value_parts = [], []
        audio_pair_sum = jnp.zeros((NA, HS), jnp.float32)
        audio_value_sum = jnp.zeros((NA, HS), jnp.float32)
        for block_index in range(N_VID):
            first_row = block_index * video_block
            row_prob, col_prob = probabilities(first_row)
            row_weight = row_prob.astype(bf_type)
            col_weight = col_prob.astype(bf_type)
            block_vpairs = head_vpairs[first_row:first_row + video_block]
            block_vvalues = head_vvalues[first_row:first_row + video_block]
            block_vback = head_vback[first_row:first_row + video_block]
            row_grad = lax.dot_general(block_vback, head_avalues, contract_last, preferred_element_type=jnp.float32)
            col_grad = lax.dot_general(block_vvalues, head_aback, contract_last, preferred_element_type=jnp.float32)
            row_delta = jnp.sum(row_prob * row_grad, axis=1, keepdims=True)
            score_grad = (row_prob * (row_grad - row_delta) + col_prob * (col_grad - col_delta[None, :])).astype(bf_type)
            video_pair_parts.append(blockwise(score_grad, head_apairs, N_AUD, audio_block, score_scale))
            video_value_parts.append(blockwise(col_weight, head_aback, N_AUD, audio_block, 1.0))
            audio_pair_sum = audio_pair_sum + transposed(score_grad, block_vpairs, score_scale)
            audio_value_sum = audio_value_sum + transposed(row_weight, block_vback, 1.0)
        video_pair_heads.append(jnp.concatenate(video_pair_parts, axis=0))
        video_value_heads.append(jnp.concatenate(video_value_parts, axis=0))
        audio_pair_heads.append(audio_pair_sum)
        audio_value_heads.append(audio_value_sum)
    video_mix = jnp.concatenate(video_mix_heads, axis=1).astype(bf_type)
    audio_mix = jnp.concatenate(audio_mix_heads, axis=1).astype(bf_type)
    video_result = jnp.dot(video_mix, video_output, preferred_element_type=jnp.float32).astype(bf_type)
    audio_result = jnp.dot(audio_mix, audio_output, preferred_element_type=jnp.float32).astype(bf_type)
    video_pair_grad = jnp.concatenate(video_pair_heads, axis=1).astype(bf_type)
    video_value_grad = jnp.concatenate(video_value_heads, axis=1).astype(bf_type)
    audio_pair_grad = jnp.concatenate(audio_pair_heads, axis=1).astype(bf_type)
    audio_value_grad = jnp.concatenate(audio_value_heads, axis=1).astype(bf_type)
    video_gradient = (lax.dot_general(video_pair_grad, pair_weight, contract_last, preferred_element_type=jnp.float32)
                      + lax.dot_general(video_value_grad, video_value, contract_last, preferred_element_type=jnp.float32)).astype(bf_type)
    audio_gradient = (lax.dot_general(audio_pair_grad, pair_weight, contract_last, preferred_element_type=jnp.float32)
                      + lax.dot_general(audio_value_grad, audio_value, contract_last, preferred_element_type=jnp.float32)).astype(bf_type)
    return video_result, audio_result, video_gradient, audio_gradient
```

```python
import functools

import jax
import jax.numpy as jnp
from jax import lax
from jax.experimental import pallas as pl
from jax.experimental.pallas import tpu as pltpu
from jax.sharding import PartitionSpec as P

HS = 128
HEADS = 2
LANES = 128
MESH = pl.DeviceIdType.MESH
BF = jnp.bfloat16
F32 = jnp.float32
SCALE = float(HS) ** -0.5
SCALE2 = SCALE * 1.4426950408889634
WIDE = 3 * HS


def product(left_side, right_side, left_dim, right_dim):
    return lax.dot_general(
        left_side,
        right_side,
        (((left_dim,), (right_dim,)), ((), ())),
        preferred_element_type=F32,
    )


def head_cols(head):
    return slice(head * HS, (head + 1) * HS)


def rounded_up(value, unit):
    return (value + unit - 1) // unit * unit


def layer_kernel(
    n_vid,
    n_aud,
    video_tokens,
    audio_tokens,
    pair_weight,
    video_value,
    audio_value,
    video_output,
    audio_output,
    video_cotangent,
    audio_cotangent,
    video_result,
    audio_result,
    video_gradient,
    audio_gradient,
    rows_in,
    pair_w,
    value_w,
    output_w,
    vown,
    aown,
    vblk,
    ablk,
    rexp,
    cexp,
    rstat,
    cstat,
    rsend,
    rrecv,
    csend,
    crecv,
    fcol,
    cfin,
    vacc,
    aacc,
    vpart,
    vrecv,
    vfar,
    apart,
    asib,
    asum,
    arecv,
    fin,
    load_sem,
    store_sem,
    vz_send,
    vz_recv,
    vx_send,
    vx_recv,
    vr_send,
    vr_recv,
    az_send,
    az_recv,
    af_send,
    af_recv,
    rs_send,
    rs_recv,
    cs_send,
    cs_recv,
    vp_send,
    vp_recv,
    vf_send,
    vf_recv,
    as_send,
    as_recv,
    ar_send,
    ar_recv,
):
    vid, aud = lax.axis_index("vid"), lax.axis_index("aud")
    n_chip, n_pair = n_aud // 2, n_vid // 2
    core, chip = lax.rem(aud, 2), aud // 2
    head, pair = lax.rem(vid, 2), vid // 2
    other = 1 - head
    partner = 2 * pair + other
    sibling = 2 * chip + 1 - core
    tv, ta = video_tokens.shape[0], audio_tokens.shape[0]
    depth = video_tokens.shape[1]
    n_tile = n_chip // 2 * 2
    half = n_chip // 2
    rows = 2 * tv
    cols = 4 * ta
    stride = rounded_up(n_tile, 8)

    def plane(dp, s):
        return 2 * lax.rem(pair + dp, n_pair) + lax.rem(head + s, 2)

    def source(dp, s):
        return 2 * lax.rem(pair + n_pair - dp, n_pair) + lax.rem(head + s, 2)

    others = [(dp, s) for dp in range(n_pair) for s in range(2) if dp or s]

    loads = []
    for i, (src, dst) in enumerate(
        (
            (pair_weight, pair_w),
            (audio_tokens, rows_in.at[1]),
            (video_tokens, rows_in.at[0]),
            (audio_value, value_w.at[1]),
            (video_value, value_w.at[0]),
            (audio_output, output_w.at[1]),
            (audio_cotangent, rows_in.at[3]),
            (video_output, output_w.at[0]),
            (video_cotangent, rows_in.at[2]),
        )
    ):
        copy = pltpu.make_async_copy(src, dst, load_sem.at[i])
        copy.start()
        loads.append(copy)

    barrier = pltpu.get_barrier_semaphore()
    count = 0
    for d in range(1, n_chip):
        pl.semaphore_signal(
            barrier,
            inc=1,
            device_id={"vid": vid, "aud": lax.rem(aud + 2 * d, n_aud)},
            device_id_type=MESH,
        )
        count += 1
    for dp, s in others:
        pl.semaphore_signal(
            barrier, inc=1, device_id={"vid": plane(dp, s), "aud": aud}, device_id_type=MESH
        )
        count += 1
    for dp in range(n_pair):
        pl.semaphore_signal(
            barrier, inc=1, device_id={"vid": plane(dp, 0), "aud": sibling}, device_id_type=MESH
        )
        count += 1

    pending = []

    def send(src, dst, send_sem, recv_sem, where):
        copy = pltpu.make_async_remote_copy(
            src_ref=src,
            dst_ref=dst,
            send_sem=send_sem,
            recv_sem=recv_sem,
            device_id={"vid": where[0], "aud": where[1]},
            device_id_type=MESH,
        )
        copy.start()
        pending.append(copy)
        return copy

    def chip_at(d):
        return (vid, lax.rem(aud + 2 * d, n_aud))

    vz, vx, vr, az, af = {}, {}, {}, {}, {}

    def put(own, k, value):
        for h in range(HEADS):
            own[h, k] = value[:, head_cols(h)].astype(BF)

    def send_near(k):
        vz[k] = send(
            vown.at[other, k], vblk.at[n_chip + chip, k], vz_send.at[k], vz_recv.at[k], (partner, aud)
        )
        for d in range(1, n_chip):
            vx[k, d] = send(
                vown.at[head, k], vblk.at[chip, k], vx_send.at[k, d], vx_recv.at[k, d], chip_at(d)
            )
        send_audio(k, 0, 1)
        af[k, 0, 0] = send(
            aown.at[head, k],
            ablk.at[pair, head, core, k],
            af_send.at[k, 0, 0],
            af_recv.at[k, 0, 0],
            (vid, sibling),
        )
        vblk[chip, k] = vown[head, k]
        ablk[pair, head, core, k] = aown[head, k]

    def send_audio(k, dp, s):
        az[k, dp, s] = send(
            aown.at[lax.rem(head + s, 2), k],
            ablk.at[pair, head, core, k],
            az_send.at[k, dp, s],
            az_recv.at[k, dp, s],
            (plane(dp, s), aud),
        )

    def relay_video(k):
        vz[k].wait_recv()
        for d in range(1, n_chip):
            vr[k, d] = send(
                vblk.at[n_chip + chip, k],
                vblk.at[n_chip + chip, k],
                vr_send.at[k, d],
                vr_recv.at[k, d],
                chip_at(d),
            )

    def relay_audio(k, dp, s):
        az[k, dp, s].wait_recv()
        z = source(dp, s)
        slot = (z // 2, lax.rem(z, 2), core, k)
        af[k, dp, s] = send(
            ablk.at[slot],
            ablk.at[slot],
            af_send.at[k, dp, s],
            af_recv.at[k, dp, s],
            (vid, sibling),
        )

    for copy in loads[:3]:
        copy.wait()
    pairs = product(rows_in[0:2].reshape(tv + ta, depth), pair_w[...], 1, 0)
    put(vown, 0, pairs[:tv])
    put(aown, 0, pairs[tv:])
    pl.semaphore_wait(barrier, count)
    send_near(0)
    for dp in range(1, n_pair):
        for s in range(2):
            send_audio(0, dp, s)
    for copy in loads[3:5]:
        copy.wait()
    put(aown, 1, product(rows_in[1], value_w[1], 1, 0))
    put(vown, 1, product(rows_in[0], value_w[0], 1, 0))
    send_near(1)
    for copy in loads[5:7]:
        copy.wait()
    put(aown, 2, product(rows_in[3], output_w[1], 1, 1))
    for copy in loads[7:9]:
        copy.wait()
    put(vown, 2, product(rows_in[2], output_w[0], 1, 1))
    send_near(2)
    for k in (1, 2):
        for dp in range(1, n_pair):
            for s in range(2):
                send_audio(k, dp, s)
    for k in range(3):
        relay_video(k)
        relay_audio(k, 0, 1)

    lane = lax.broadcasted_iota(jnp.int32, (rows, LANES), 1)

    def audio_side(dp, k):
        return ablk[lax.rem(pair + dp, n_pair), :, :, k].reshape(cols, HS)

    def video_side(tile, k):
        return vblk[pl.ds(2 * tile, 2), k].reshape(rows, HS)

    def by_eight(value):
        return value.reshape(rows // 8, 8, cols)

    def stat_tiles(dp, role):
        def step(m, carry):
            tile = role * half + m
            s = SCALE2 * product(video_side(tile, 0), audio_side(dp, 0), 1, 1)
            row_peak = jnp.max(s, axis=1, keepdims=True)
            col_peak = jnp.max(by_eight(s), axis=0)
            row_exp = jnp.exp2(s - row_peak)
            col_exp = jnp.exp2(by_eight(s) - col_peak[None])
            row_grad = product(video_side(tile, 2), audio_side(dp, 1), 1, 1)
            col_grad = product(video_side(tile, 1), audio_side(dp, 2), 1, 1)
            cstat[0, dp, tile] = col_peak
            cstat[1, dp, tile] = jnp.sum(col_exp, axis=0)
            cstat[2, dp, tile] = jnp.sum(col_exp * by_eight(col_grad), axis=0)
            rexp[dp, tile] = row_exp.astype(rexp.dtype)
            cexp[dp, tile] = col_exp.reshape(rows, cols).astype(cexp.dtype)
            row_total = jnp.sum(row_exp, axis=1, keepdims=True)
            row_dot = jnp.sum(row_exp * row_grad, axis=1, keepdims=True)
            for k, value in enumerate((row_peak, row_total, row_dot)):
                rstat[k] = jnp.where(lane == dp * stride + tile, value, rstat[k])
            return carry

        lax.fori_loop(0, half, step, 0)

    rstat[...] = jnp.zeros_like(rstat)
    for k in range(3):
        for d in range(1, n_chip):
            vx[k, d].wait_recv()
        af[k, 0, 0].wait_recv()
        af[k, 0, 1].wait_recv()
    stat_tiles(0, 0)
    for k in range(3):
        for dp in range(1, n_pair):
            for s in range(2):
                relay_audio(k, dp, s)
    for k in range(3):
        for d in range(1, n_chip):
            vr[k, d].wait_recv()
    stat_tiles(0, 1)
    for dp in range(1, n_pair):
        for k in range(3):
            for s in range(2):
                af[k, dp, s].wait_recv()
        for role in (0, 1):
            stat_tiles(dp, role)

    def combine(parts):
        top = functools.reduce(jnp.maximum, [part[0] for part in parts])
        gains = [jnp.exp2(part[0] - top) for part in parts]
        total = sum(part[1] * gain for part, gain in zip(parts, gains))
        dots = sum(part[2] * gain for part, gain in zip(parts, gains))
        return top, total, dots

    rows_t = [rstat[k].T for k in range(3)]
    row_parts = [
        [rows_t[k][dp * stride : (dp + 1) * stride] for k in range(3)] for dp in range(n_pair)
    ]
    for k, value in enumerate(combine(row_parts)):
        rsend[k] = value
    rs = {}
    for d in range(1, n_chip):
        rs[d] = send(rsend, rrecv.at[d], rs_send.at[d], rs_recv.at[d], chip_at(d))
    for dp in range(n_pair):
        peak = cstat[0, dp]
        top = jnp.max(jnp.max(peak, axis=0), axis=0, keepdims=True)
        gain = jnp.exp2(peak - top[None])
        where = lax.rem(pair + dp, n_pair)
        csend[0, where] = top
        for k in (1, 2):
            csend[k, where] = jnp.sum(jnp.sum(cstat[k, dp] * gain, axis=0), axis=0, keepdims=True)
    cs = {}
    for dp in range(n_pair):
        for c in range(2):
            if dp or c:
                cs[dp, c] = send(
                    csend,
                    crecv.at[dp, c],
                    cs_send.at[dp, c],
                    cs_recv.at[dp, c],
                    (plane(dp, 0), sibling if c else aud),
                )
    for d in range(1, n_chip):
        rs[d].wait_recv()
    top, total, dots = combine(
        [[rsend[k] for k in range(3)]]
        + [[rrecv[d, k] for k in range(3)] for d in range(1, n_chip)]
    )
    factors = [jnp.exp2(part[0] - top) / total for part in row_parts] + [dots / total]
    blank = jnp.zeros((LANES - stride * (n_pair + 1), rows), F32)
    fcol[...] = jnp.concatenate(factors + [blank], axis=0).T
    for copy in cs.values():
        copy.wait_recv()
    col_top, col_total, col_dots = combine(
        [[csend[k] for k in range(3)]] + [[crecv[key + (k,)] for k in range(3)] for key in cs]
    )
    cfin[0] = col_top
    cfin[1] = 1.0 / col_total
    cfin[2] = col_dots / col_total

    order = list(range(1, n_pair)) + [0]
    vp = {}

    def column(t):
        return jnp.sum(jnp.where(lane == t, fcol[...], 0.0), axis=1, keepdims=True)

    def grad_tile(dp, j):
        tile = lax.rem(j + half, n_tile)
        where = lax.rem(pair + dp, n_pair)
        vpairs, vvalues, vback = (video_side(tile, k) for k in range(3))
        apairs, avalues, aback = (audio_side(dp, k) for k in range(3))
        row_gain = column(dp * stride + tile)
        row_delta = column(n_pair * stride + tile)
        col_gain = jnp.exp2(cstat[0, dp, tile] - cfin[0, where]) * cfin[1, where]
        col_delta = cfin[2, where]
        row_prob = rexp[dp, tile].astype(F32) * row_gain
        col_prob = (by_eight(cexp[dp, tile].astype(F32)) * col_gain[None]).reshape(rows, cols)
        row_weight, col_weight = row_prob.astype(BF), col_prob.astype(BF)
        row_grad = product(vback, avalues, 1, 1)
        col_grad = product(vvalues, aback, 1, 1)
        score_grad = (
            row_prob * (row_grad - row_delta) + col_prob * (col_grad - col_delta)
        ).astype(BF)
        for k, (left, right) in enumerate(
            ((row_weight, avalues), (score_grad, apairs), (col_weight, aback))
        ):
            part = product(left, right, 1, 0)
            if dp != order[0]:
                part += vacc[tile, :, head_cols(k)]
            if dp != order[-1]:
                vacc[tile, :, head_cols(k)] = part
            else:
                if k == 1:
                    part = SCALE * part
                vpart[pl.ds(2 * tile, 2), :, head_cols(k)] = part.reshape(2, tv, HS).astype(BF)
        for k, (left, right) in enumerate(
            ((vvalues, col_weight), (vpairs, score_grad), (vback, row_weight))
        ):
            aacc[head_cols(k)] += product(left, right, 0, 0)
        if dp == order[-1]:
            for e in range(2):
                block = 2 * tile + e
                owner = lax.rem(block, n_chip)

                @pl.when(owner != chip)
                def _(block=block, owner=owner):
                    pltpu.make_async_remote_copy(
                        src_ref=vpart.at[block],
                        dst_ref=vrecv.at[(block // n_chip) * n_chip + chip],
                        send_sem=vp_send.at[block],
                        recv_sem=vp_recv.at[(block // n_chip) * n_chip + chip],
                        device_id={"vid": vid, "aud": 2 * owner + core},
                        device_id_type=MESH,
                    ).start()

    siblings, ar = {}, {}

    def share_audio(dp):
        for s in range(2):
            for c in range(2):
                piece = slice((2 * s + c) * ta, (2 * s + c + 1) * ta)
                for k in range(3):
                    value = aacc[head_cols(k), piece]
                    apart[dp, c, s, head_cols(k)] = (SCALE * value if k == 1 else value).astype(BF)
        siblings[dp] = send(
            apart.at[dp, 1 - core], asib.at[dp], as_send.at[dp], as_recv.at[dp], (vid, sibling)
        )

    def reduce_audio(dp):
        siblings[dp].wait_recv()
        for s in range(2):
            which = lax.rem(head + s, 2)
            both = apart[dp, core, which].astype(F32) + asib[dp, which].astype(F32)
            asum[dp, s] = both.astype(BF)
            if dp or s:
                ar[dp, s] = send(
                    asum.at[dp, s],
                    arecv.at[dp, s],
                    ar_send.at[dp, s],
                    ar_recv.at[dp, s],
                    (plane(dp, s), aud),
                )

    for index, dp in enumerate(order):
        aacc[...] = jnp.zeros_like(aacc)

        def step(j, carry, dp=dp):
            grad_tile(dp, j)
            return carry

        if index:
            lax.fori_loop(0, 1, step, 0)
            reduce_audio(order[index - 1])
        lax.fori_loop(1 if index else 0, n_tile, step, 0)
        share_audio(dp)

    def video_parts(role):
        for d in range(1, n_chip):
            slot = role * n_chip + lax.rem(chip + d, n_chip)
            pltpu.make_async_remote_copy(
                src_ref=vpart.at[slot],
                dst_ref=vrecv.at[slot],
                send_sem=vp_send.at[slot],
                recv_sem=vp_recv.at[slot],
                device_id={"vid": vid, "aud": chip_at(d)[1]},
                device_id_type=MESH,
            ).wait()
        total = vpart[role * n_chip + chip].astype(F32)
        for d in range(1, n_chip):
            total += vrecv[role * n_chip + lax.rem(chip + d, n_chip)].astype(F32)
        return total.astype(BF)

    reduce_audio(order[-1])
    vfar[0] = video_parts(1)
    far = send(vfar.at[0], vfar.at[1], vf_send.at[0], vf_recv.at[0], (partner, aud))
    fin[0, head] = video_parts(0)
    far.wait_recv()
    fin[0, other] = vfar[1]

    stores = []
    span = min(depth, 1024)

    def results(side, result, gradient):
        mix, pairs, values = (
            jnp.concatenate([fin[side, h, :, head_cols(k)] for h in range(HEADS)], axis=1)
            for k in range(3)
        )
        for n in range(depth // span):
            part = slice(n * span, (n + 1) * span)
            rows_in[side, :, part] = product(mix, output_w[side, :, part], 1, 0).astype(BF)
            rows_in[2 + side, :, part] = (
                product(pairs, pair_w[part], 1, 1) + product(values, value_w[side, part], 1, 1)
            ).astype(BF)
            for i, out in enumerate((result, gradient)):
                copy = pltpu.make_async_copy(
                    rows_in.at[side + 2 * i, :, part], out.at[:, part], store_sem.at[side, i, n]
                )
                copy.start()
                stores.append(copy)

    results(0, video_result, video_gradient)
    for copy in ar.values():
        copy.wait_recv()
    mine, theirs = asum[0, 0].astype(F32), arecv[0, 1].astype(F32)
    for dp in range(1, n_pair):
        mine += arecv[dp, 0].astype(F32)
        theirs += arecv[dp, 1].astype(F32)
    fin[1, head] = mine.T.astype(BF)
    fin[1, other] = theirs.T.astype(BF)
    results(1, audio_result, audio_gradient)
    for copy in pending:
        copy.wait_send()
    for copy in stores:
        copy.wait()


def on_device(n_vid, n_aud, *arrays):
    tv, depth = arrays[0].shape
    ta = arrays[1].shape[0]
    hd = arrays[2].shape[1]
    n_chip, n_pair = n_aud // 2, n_vid // 2
    n_tile = n_chip
    rows, cols = 2 * tv, 4 * ta
    stride = rounded_up(n_tile, 8)
    dma = pltpu.SemaphoreType.DMA
    kept = F32 if n_pair * n_tile * rows * cols <= 2**21 else BF
    remote = [
        (3,),
        (3, n_chip),
        (3, n_chip),
        (3, n_pair, 2),
        (3, n_pair, 2),
        (n_chip,),
        (n_pair, 2),
        (2 * n_chip,),
        (1,),
        (n_pair,),
        (n_pair, 2),
    ]
    outs = (
        jax.ShapeDtypeStruct((tv, depth), BF),
        jax.ShapeDtypeStruct((ta, depth), BF),
        jax.ShapeDtypeStruct((tv, depth), BF),
        jax.ShapeDtypeStruct((ta, depth), BF),
    )
    return pl.pallas_call(
        functools.partial(layer_kernel, n_vid, n_aud),
        out_shape=outs,
        in_specs=[pl.BlockSpec(memory_space=pl.ANY)] * 9,
        out_specs=(pl.BlockSpec(memory_space=pl.ANY),) * 4,
        scratch_shapes=[
            pltpu.VMEM((4, tv, depth), BF),
            pltpu.VMEM((depth, hd), BF),
            pltpu.VMEM((2, depth, hd), BF),
            pltpu.VMEM((2, hd, depth), BF),
            pltpu.VMEM((HEADS, 3, tv, HS), BF),
            pltpu.VMEM((HEADS, 3, ta, HS), BF),
            pltpu.VMEM((2 * n_chip, 3, tv, HS), BF),
            pltpu.VMEM((n_pair, 2, 2, 3, ta, HS), BF),
            pltpu.VMEM((n_pair, n_tile, rows, cols), kept),
            pltpu.VMEM((n_pair, n_tile, rows, cols), kept),
            pltpu.VMEM((3, rows, LANES), F32),
            pltpu.VMEM((3, n_pair, n_tile, 8, cols), F32),
            pltpu.VMEM((3, stride, rows), F32),
            pltpu.VMEM((n_chip, 3, stride, rows), F32),
            pltpu.VMEM((3, n_pair, 1, cols), F32),
            pltpu.VMEM((n_pair, 2, 3, n_pair, 1, cols), F32),
            pltpu.VMEM((rows, LANES), F32),
            pltpu.VMEM((3, n_pair, 1, cols), F32),
            pltpu.VMEM((n_tile, rows, WIDE), F32),
            pltpu.VMEM((WIDE, cols), F32),
            pltpu.VMEM((2 * n_chip, tv, WIDE), BF),
            pltpu.VMEM((2 * n_chip, tv, WIDE), BF),
            pltpu.VMEM((2, tv, WIDE), BF),
            pltpu.VMEM((n_pair, 2, 2, WIDE, ta), BF),
            pltpu.VMEM((n_pair, 2, WIDE, ta), BF),
            pltpu.VMEM((n_pair, 2, WIDE, ta), BF),
            pltpu.VMEM((n_pair, 2, WIDE, ta), BF),
            pltpu.VMEM((2, HEADS, tv, WIDE), BF),
            dma((9,)),
            dma((2, 2, max(1, depth // 1024))),
        ]
        + [dma(shape) for shape in remote for _ in range(2)],
        compiler_params=pltpu.CompilerParams(
            collective_id=0, has_side_effects=True, vmem_limit_bytes=60 * 1024 * 1024
        ),
    )(*arrays)


def solution(mesh):
    rows_v, rows_a = P(("vid", "aud"), None), P(("aud", "vid"), None)
    return jax.shard_map(
        functools.partial(on_device, mesh.shape["vid"], mesh.shape["aud"]),
        mesh=mesh,
        in_specs=(rows_v, rows_a, P(), P(), P(), P(), P(), rows_v, rows_a),
        out_specs=(rows_v, rows_a, rows_v, rows_a),
        check_vma=False,
    )
```

```python
import functools

import jax
import jax.numpy as jnp
from jax import lax
from jax.experimental import pallas as pl
from jax.experimental.pallas import tpu as pltpu
from jax.sharding import PartitionSpec as P

HS = 128
HEADS = 2
LANES = 128
MESH = pl.DeviceIdType.MESH
BF = jnp.bfloat16
F32 = jnp.float32
SCALE = float(HS) ** -0.5
SCALE2 = SCALE * 1.4426950408889634
WIDE = 3 * HS


def product(left_side, right_side, left_dim, right_dim):
    return lax.dot_general(
        left_side,
        right_side,
        (((left_dim,), (right_dim,)), ((), ())),
        preferred_element_type=F32,
    )


def head_cols(head):
    return slice(head * HS, (head + 1) * HS)


def rounded_up(value, unit):
    return (value + unit - 1) // unit * unit


def layer_kernel(
    n_vid,
    n_aud,
    video_tokens,
    audio_tokens,
    pair_weight,
    video_value,
    audio_value,
    video_output,
    audio_output,
    video_cotangent,
    audio_cotangent,
    video_rows,
    audio_fin,
    pair_w,
    value_a,
    output_a,
    rows_in,
    value_v,
    output_v,
    vown,
    aown,
    vblk,
    ablk,
    rexp,
    cexp,
    rstat,
    cstat,
    rsend,
    rrecv,
    csend,
    crecv,
    fcol,
    cfin,
    vacc,
    aacc,
    vpart,
    vrecv,
    vfar,
    apart,
    asib,
    asum,
    arecv,
    fin,
    load_sem,
    vz_send,
    vz_recv,
    vx_send,
    vx_recv,
    vr_send,
    vr_recv,
    az_send,
    az_recv,
    af_send,
    af_recv,
    rs_send,
    rs_recv,
    cs_send,
    cs_recv,
    vp_send,
    vp_recv,
    vf_send,
    vf_recv,
    as_send,
    as_recv,
    ar_send,
    ar_recv,
):
    vid, aud = lax.axis_index("vid"), lax.axis_index("aud")
    n_chip, n_pair = n_aud // 2, n_vid // 2
    core, chip = lax.rem(aud, 2), aud // 2
    head, pair = lax.rem(vid, 2), vid // 2
    other = 1 - head
    partner = 2 * pair + other
    sibling = 2 * chip + 1 - core
    tv, ta = video_tokens.shape[0], audio_tokens.shape[0]
    depth = video_tokens.shape[1]
    n_tile = n_chip // 2 * 2
    half = n_chip // 2
    rows = 2 * tv
    cols = 4 * ta
    stride = rounded_up(n_tile, 8)

    def plane(dp, s):
        return 2 * lax.rem(pair + dp, n_pair) + lax.rem(head + s, 2)

    def source(dp, s):
        return 2 * lax.rem(pair + n_pair - dp, n_pair) + lax.rem(head + s, 2)

    others = [(dp, s) for dp in range(n_pair) for s in range(2) if dp or s]

    loads = []
    for i, (src, dst) in enumerate(
        (
            (pair_weight, pair_w),
            (audio_tokens, rows_in.at[1]),
            (video_tokens, rows_in.at[0]),
            (audio_value, value_a),
            (video_value, value_v),
            (audio_output, output_a),
            (audio_cotangent, rows_in.at[3]),
            (video_output, output_v),
            (video_cotangent, rows_in.at[2]),
        )
    ):
        copy = pltpu.make_async_copy(src, dst, load_sem.at[i])
        copy.start()
        loads.append(copy)

    barrier = pltpu.get_barrier_semaphore()
    count = 0
    for d in range(1, n_chip):
        pl.semaphore_signal(
            barrier,
            inc=1,
            device_id={"vid": vid, "aud": lax.rem(aud + 2 * d, n_aud)},
            device_id_type=MESH,
        )
        count += 1
    for dp, s in others:
        pl.semaphore_signal(
            barrier, inc=1, device_id={"vid": plane(dp, s), "aud": aud}, device_id_type=MESH
        )
        count += 1
    for dp in range(n_pair):
        pl.semaphore_signal(
            barrier, inc=1, device_id={"vid": plane(dp, 0), "aud": sibling}, device_id_type=MESH
        )
        count += 1

    pending = []

    def send(src, dst, send_sem, recv_sem, where):
        copy = pltpu.make_async_remote_copy(
            src_ref=src,
            dst_ref=dst,
            send_sem=send_sem,
            recv_sem=recv_sem,
            device_id={"vid": where[0], "aud": where[1]},
            device_id_type=MESH,
        )
        copy.start()
        pending.append(copy)
        return copy

    def chip_at(d):
        return (vid, lax.rem(aud + 2 * d, n_aud))

    vz, vx, vr, az, af = {}, {}, {}, {}, {}

    def put(own, k, value):
        for h in range(HEADS):
            own[h, k] = value[:, head_cols(h)].astype(BF)

    def send_near(k):
        vz[k] = send(
            vown.at[other, k], vblk.at[n_chip + chip, k], vz_send.at[k], vz_recv.at[k], (partner, aud)
        )
        for d in range(1, n_chip):
            vx[k, d] = send(
                vown.at[head, k], vblk.at[chip, k], vx_send.at[k, d], vx_recv.at[k, d], chip_at(d)
            )
        send_audio(k, 0, 1)
        af[k, 0, 0] = send(
            aown.at[head, k],
            ablk.at[pair, head, core, k],
            af_send.at[k, 0, 0],
            af_recv.at[k, 0, 0],
            (vid, sibling),
        )
        vblk[chip, k] = vown[head, k]
        ablk[pair, head, core, k] = aown[head, k]

    def send_audio(k, dp, s):
        az[k, dp, s] = send(
            aown.at[lax.rem(head + s, 2), k],
            ablk.at[pair, head, core, k],
            az_send.at[k, dp, s],
            az_recv.at[k, dp, s],
            (plane(dp, s), aud),
        )

    def relay_video(k):
        vz[k].wait_recv()
        for d in range(1, n_chip):
            vr[k, d] = send(
                vblk.at[n_chip + chip, k],
                vblk.at[n_chip + chip, k],
                vr_send.at[k, d],
                vr_recv.at[k, d],
                chip_at(d),
            )

    def relay_audio(k, dp, s):
        az[k, dp, s].wait_recv()
        z = source(dp, s)
        slot = (z // 2, lax.rem(z, 2), core, k)
        af[k, dp, s] = send(
            ablk.at[slot],
            ablk.at[slot],
            af_send.at[k, dp, s],
            af_recv.at[k, dp, s],
            (vid, sibling),
        )

    for copy in loads[:3]:
        copy.wait()
    pairs = product(rows_in[0:2].reshape(tv + ta, depth), pair_w[...], 1, 0)
    put(vown, 0, pairs[:tv])
    put(aown, 0, pairs[tv:])
    pl.semaphore_wait(barrier, count)
    send_near(0)
    for dp in range(1, n_pair):
        for s in range(2):
            send_audio(0, dp, s)
    for copy in loads[3:5]:
        copy.wait()
    put(aown, 1, product(rows_in[1], value_a[...], 1, 0))
    put(vown, 1, product(rows_in[0], value_v[...], 1, 0))
    send_near(1)
    for copy in loads[5:7]:
        copy.wait()
    put(aown, 2, product(rows_in[3], output_a[...], 1, 1))
    for copy in loads[7:9]:
        copy.wait()
    put(vown, 2, product(rows_in[2], output_v[...], 1, 1))
    send_near(2)
    for k in (1, 2):
        for dp in range(1, n_pair):
            for s in range(2):
                send_audio(k, dp, s)
    for k in range(3):
        relay_video(k)
        relay_audio(k, 0, 1)

    lane = lax.broadcasted_iota(jnp.int32, (rows, LANES), 1)

    def audio_side(dp, k):
        return ablk[lax.rem(pair + dp, n_pair), :, :, k].reshape(cols, HS)

    def video_side(tile, k):
        return vblk[pl.ds(2 * tile, 2), k].reshape(rows, HS)

    def by_eight(value):
        return value.reshape(rows // 8, 8, cols)

    def stat_tiles(dp, role):
        def step(m, carry):
            tile = role * half + m
            s = SCALE2 * product(video_side(tile, 0), audio_side(dp, 0), 1, 1)
            row_peak = jnp.max(s, axis=1, keepdims=True)
            col_peak = jnp.max(by_eight(s), axis=0)
            row_exp = jnp.exp2(s - row_peak)
            col_exp = jnp.exp2(by_eight(s) - col_peak[None])
            row_grad = product(video_side(tile, 2), audio_side(dp, 1), 1, 1)
            col_grad = product(video_side(tile, 1), audio_side(dp, 2), 1, 1)
            cstat[0, dp, tile] = col_peak
            cstat[1, dp, tile] = jnp.sum(col_exp, axis=0)
            cstat[2, dp, tile] = jnp.sum(col_exp * by_eight(col_grad), axis=0)
            rexp[dp, tile] = row_exp.astype(rexp.dtype)
            cexp[dp, tile] = col_exp.reshape(rows, cols).astype(cexp.dtype)
            row_total = jnp.sum(row_exp, axis=1, keepdims=True)
            row_dot = jnp.sum(row_exp * row_grad, axis=1, keepdims=True)
            for k, value in enumerate((row_peak, row_total, row_dot)):
                rstat[k] = jnp.where(lane == dp * stride + tile, value, rstat[k])
            return carry

        lax.fori_loop(0, half, step, 0)

    rstat[...] = jnp.zeros_like(rstat)
    for k in range(3):
        for d in range(1, n_chip):
            vx[k, d].wait_recv()
        af[k, 0, 0].wait_recv()
        af[k, 0, 1].wait_recv()
    stat_tiles(0, 0)
    for k in range(3):
        for dp in range(1, n_pair):
            for s in range(2):
                relay_audio(k, dp, s)
    for k in range(3):
        for d in range(1, n_chip):
            vr[k, d].wait_recv()
    stat_tiles(0, 1)
    for dp in range(1, n_pair):
        for k in range(3):
            for s in range(2):
                af[k, dp, s].wait_recv()
        for role in (0, 1):
            stat_tiles(dp, role)

    def combine(parts):
        top = functools.reduce(jnp.maximum, [part[0] for part in parts])
        gains = [jnp.exp2(part[0] - top) for part in parts]
        total = sum(part[1] * gain for part, gain in zip(parts, gains))
        dots = sum(part[2] * gain for part, gain in zip(parts, gains))
        return top, total, dots

    rows_t = [rstat[k].T for k in range(3)]
    row_parts = [
        [rows_t[k][dp * stride : (dp + 1) * stride] for k in range(3)] for dp in range(n_pair)
    ]
    for k, value in enumerate(combine(row_parts)):
        rsend[k] = value
    rs = {}
    for d in range(1, n_chip):
        rs[d] = send(rsend, rrecv.at[d], rs_send.at[d], rs_recv.at[d], chip_at(d))
    for dp in range(n_pair):
        peak = cstat[0, dp]
        top = jnp.max(jnp.max(peak, axis=0), axis=0, keepdims=True)
        gain = jnp.exp2(peak - top[None])
        where = lax.rem(pair + dp, n_pair)
        csend[0, where] = top
        for k in (1, 2):
            csend[k, where] = jnp.sum(jnp.sum(cstat[k, dp] * gain, axis=0), axis=0, keepdims=True)
    cs = {}
    for dp in range(n_pair):
        for c in range(2):
            if dp or c:
                cs[dp, c] = send(
                    csend,
                    crecv.at[dp, c],
                    cs_send.at[dp, c],
                    cs_recv.at[dp, c],
                    (plane(dp, 0), sibling if c else aud),
                )
    for d in range(1, n_chip):
        rs[d].wait_recv()
    top, total, dots = combine(
        [[rsend[k] for k in range(3)]]
        + [[rrecv[d, k] for k in range(3)] for d in range(1, n_chip)]
    )
    factors = [jnp.exp2(part[0] - top) / total for part in row_parts] + [dots / total]
    blank = jnp.zeros((LANES - stride * (n_pair + 1), rows), F32)
    fcol[...] = jnp.concatenate(factors + [blank], axis=0).T
    for copy in cs.values():
        copy.wait_recv()
    col_top, col_total, col_dots = combine(
        [[csend[k] for k in range(3)]] + [[crecv[key + (k,)] for k in range(3)] for key in cs]
    )
    cfin[0] = col_top
    cfin[1] = 1.0 / col_total
    cfin[2] = col_dots / col_total

    order = list(range(1, n_pair)) + [0]
    vp = {}

    def column(t):
        return jnp.sum(jnp.where(lane == t, fcol[...], 0.0), axis=1, keepdims=True)

    def grad_tile(dp, j):
        tile = lax.rem(j + half, n_tile)
        where = lax.rem(pair + dp, n_pair)
        vpairs, vvalues, vback = (video_side(tile, k) for k in range(3))
        apairs, avalues, aback = (audio_side(dp, k) for k in range(3))
        row_gain = column(dp * stride + tile)
        row_delta = column(n_pair * stride + tile)
        col_gain = jnp.exp2(cstat[0, dp, tile] - cfin[0, where]) * cfin[1, where]
        col_delta = cfin[2, where]
        row_prob = rexp[dp, tile].astype(F32) * row_gain
        col_prob = (by_eight(cexp[dp, tile].astype(F32)) * col_gain[None]).reshape(rows, cols)
        row_weight, col_weight = row_prob.astype(BF), col_prob.astype(BF)
        row_grad = product(vback, avalues, 1, 1)
        col_grad = product(vvalues, aback, 1, 1)
        score_grad = (
            row_prob * (row_grad - row_delta) + col_prob * (col_grad - col_delta)
        ).astype(BF)
        for k, (left, right) in enumerate(
            ((row_weight, avalues), (score_grad, apairs), (col_weight, aback))
        ):
            part = product(left, right, 1, 0)
            if dp != order[0]:
                part += vacc[tile, :, head_cols(k)]
            if dp != order[-1]:
                vacc[tile, :, head_cols(k)] = part
            else:
                if k == 1:
                    part = SCALE * part
                vpart[pl.ds(2 * tile, 2), :, head_cols(k)] = part.reshape(2, tv, HS).astype(BF)
        for k, (left, right) in enumerate(
            ((vvalues, col_weight), (vpairs, score_grad), (vback, row_weight))
        ):
            aacc[head_cols(k)] += product(left, right, 0, 0)
        if dp == order[-1]:
            for e in range(2):
                block = 2 * tile + e
                owner = lax.rem(block, n_chip)

                @pl.when(owner != chip)
                def _(block=block, owner=owner):
                    pltpu.make_async_remote_copy(
                        src_ref=vpart.at[block],
                        dst_ref=vrecv.at[(block // n_chip) * n_chip + chip],
                        send_sem=vp_send.at[block],
                        recv_sem=vp_recv.at[(block // n_chip) * n_chip + chip],
                        device_id={"vid": vid, "aud": 2 * owner + core},
                        device_id_type=MESH,
                    ).start()

    siblings, ar = {}, {}

    def share_audio(dp):
        for s in range(2):
            for c in range(2):
                piece = slice((2 * s + c) * ta, (2 * s + c + 1) * ta)
                for k in range(3):
                    value = aacc[head_cols(k), piece]
                    apart[dp, c, s, head_cols(k)] = (SCALE * value if k == 1 else value).astype(BF)
        siblings[dp] = send(
            apart.at[dp, 1 - core], asib.at[dp], as_send.at[dp], as_recv.at[dp], (vid, sibling)
        )

    def reduce_audio(dp):
        siblings[dp].wait_recv()
        for s in range(2):
            which = lax.rem(head + s, 2)
            both = apart[dp, core, which].astype(F32) + asib[dp, which].astype(F32)
            asum[dp, s] = both.astype(BF)
            if dp or s:
                ar[dp, s] = send(
                    asum.at[dp, s],
                    arecv.at[dp, s],
                    ar_send.at[dp, s],
                    ar_recv.at[dp, s],
                    (plane(dp, s), aud),
                )

    for index, dp in enumerate(order):
        aacc[...] = jnp.zeros_like(aacc)

        def step(j, carry, dp=dp):
            grad_tile(dp, j)
            return carry

        if index:
            lax.fori_loop(0, 1, step, 0)
            reduce_audio(order[index - 1])
        lax.fori_loop(1 if index else 0, n_tile, step, 0)
        share_audio(dp)

    def video_parts(role):
        for d in range(1, n_chip):
            slot = role * n_chip + lax.rem(chip + d, n_chip)
            pltpu.make_async_remote_copy(
                src_ref=vpart.at[slot],
                dst_ref=vrecv.at[slot],
                send_sem=vp_send.at[slot],
                recv_sem=vp_recv.at[slot],
                device_id={"vid": vid, "aud": chip_at(d)[1]},
                device_id_type=MESH,
            ).wait()
        total = vpart[role * n_chip + chip].astype(F32)
        for d in range(1, n_chip):
            total += vrecv[role * n_chip + lax.rem(chip + d, n_chip)].astype(F32)
        return total.astype(BF)

    reduce_audio(order[-1])
    vfar[0] = video_parts(1)
    far = send(vfar.at[0], vfar.at[1], vf_send.at[0], vf_recv.at[0], (partner, aud))
    fin[head] = video_parts(0)
    far.wait_recv()
    fin[other] = vfar[1]
    for part, result, gradient in output_parts(fin, output_v, pair_w, value_v):
        video_rows[0, :, part] = result
        video_rows[1, :, part] = gradient
    for copy in ar.values():
        copy.wait_recv()
    mine, theirs = asum[0, 0].astype(F32), arecv[0, 1].astype(F32)
    for dp in range(1, n_pair):
        mine += arecv[dp, 0].astype(F32)
        theirs += arecv[dp, 1].astype(F32)
    audio_fin[head] = mine.T.astype(BF)
    audio_fin[other] = theirs.T.astype(BF)
    for copy in pending:
        copy.wait_send()


def output_parts(fin, output_w, pair_w, value_w):
    mix, pairs, values = (
        jnp.concatenate([fin[h, :, head_cols(k)] for h in range(HEADS)], axis=1) for k in range(3)
    )
    depth = pair_w.shape[0]
    span = min(depth, 1024)
    for n in range(depth // span):
        part = slice(n * span, (n + 1) * span)
        yield (
            part,
            product(mix, output_w[:, part], 1, 0).astype(BF),
            (product(pairs, pair_w[part], 1, 1) + product(values, value_w[part], 1, 1)).astype(BF),
        )


def output_kernel(
    video_rows,
    audio_fin,
    pair_w,
    value_a,
    output_a,
    video_result,
    audio_result,
    video_gradient,
    audio_gradient,
    audio_rows,
    video_sem,
    audio_sem,
):
    stores = []

    def store(src, dst, sem):
        copy = pltpu.make_async_copy(src, dst, sem)
        copy.start()
        stores.append(copy)

    for i, out in enumerate((video_result, video_gradient)):
        store(video_rows.at[i], out, video_sem.at[i])
    for n, (part, *values) in enumerate(output_parts(audio_fin, output_a, pair_w, value_a)):
        for i, out in enumerate((audio_result, audio_gradient)):
            audio_rows[i, :, part] = values[i]
            store(audio_rows.at[i, :, part], out.at[:, part], audio_sem.at[i, n])
    for copy in stores:
        copy.wait()


def on_device(n_vid, n_aud, *arrays):
    tv, depth = arrays[0].shape
    ta = arrays[1].shape[0]
    hd = arrays[2].shape[1]
    n_chip, n_pair = n_aud // 2, n_vid // 2
    n_tile = n_chip
    rows, cols = 2 * tv, 4 * ta
    stride = rounded_up(n_tile, 8)
    dma = pltpu.SemaphoreType.DMA
    kept = F32 if n_pair * n_tile * rows * cols <= 2**21 else BF
    remote = [
        (3,),
        (3, n_chip),
        (3, n_chip),
        (3, n_pair, 2),
        (3, n_pair, 2),
        (n_chip,),
        (n_pair, 2),
        (2 * n_chip,),
        (1,),
        (n_pair,),
        (n_pair, 2),
    ]
    video_out = jax.ShapeDtypeStruct((tv, depth), BF)
    audio_out = jax.ShapeDtypeStruct((ta, depth), BF)
    vmem = pl.BlockSpec(memory_space=pltpu.VMEM)
    anywhere = pl.BlockSpec(memory_space=pl.ANY)
    held = pl.pallas_call(
        functools.partial(layer_kernel, n_vid, n_aud),
        out_shape=(
            pltpu.VMEM((2, tv, depth), BF),
            pltpu.VMEM((HEADS, ta, WIDE), BF),
            pltpu.VMEM((depth, hd), BF),
            pltpu.VMEM((depth, hd), BF),
            pltpu.VMEM((hd, depth), BF),
        ),
        in_specs=[anywhere] * 9,
        out_specs=(vmem,) * 5,
        scratch_shapes=[
            pltpu.VMEM((4, tv, depth), BF),
            pltpu.VMEM((depth, hd), BF),
            pltpu.VMEM((hd, depth), BF),
            pltpu.VMEM((HEADS, 3, tv, HS), BF),
            pltpu.VMEM((HEADS, 3, ta, HS), BF),
            pltpu.VMEM((2 * n_chip, 3, tv, HS), BF),
            pltpu.VMEM((n_pair, 2, 2, 3, ta, HS), BF),
            pltpu.VMEM((n_pair, n_tile, rows, cols), kept),
            pltpu.VMEM((n_pair, n_tile, rows, cols), kept),
            pltpu.VMEM((3, rows, LANES), F32),
            pltpu.VMEM((3, n_pair, n_tile, 8, cols), F32),
            pltpu.VMEM((3, stride, rows), F32),
            pltpu.VMEM((n_chip, 3, stride, rows), F32),
            pltpu.VMEM((3, n_pair, 1, cols), F32),
            pltpu.VMEM((n_pair, 2, 3, n_pair, 1, cols), F32),
            pltpu.VMEM((rows, LANES), F32),
            pltpu.VMEM((3, n_pair, 1, cols), F32),
            pltpu.VMEM((n_tile, rows, WIDE), F32),
            pltpu.VMEM((WIDE, cols), F32),
            pltpu.VMEM((2 * n_chip, tv, WIDE), BF),
            pltpu.VMEM((2 * n_chip, tv, WIDE), BF),
            pltpu.VMEM((2, tv, WIDE), BF),
            pltpu.VMEM((n_pair, 2, 2, WIDE, ta), BF),
            pltpu.VMEM((n_pair, 2, WIDE, ta), BF),
            pltpu.VMEM((n_pair, 2, WIDE, ta), BF),
            pltpu.VMEM((n_pair, 2, WIDE, ta), BF),
            pltpu.VMEM((HEADS, tv, WIDE), BF),
            dma((9,)),
        ]
        + [dma(shape) for shape in remote for _ in range(2)],
        compiler_params=pltpu.CompilerParams(
            collective_id=0, has_side_effects=True, vmem_limit_bytes=50 * 1024 * 1024
        ),
    )(*(pltpu.with_memory_space_constraint(array, pltpu.HBM) for array in arrays))
    return pl.pallas_call(
        output_kernel,
        out_shape=(video_out, audio_out, video_out, audio_out),
        in_specs=[vmem] * 5,
        out_specs=(anywhere,) * 4,
        scratch_shapes=[
            pltpu.VMEM((2, ta, depth), BF),
            dma((2,)),
            dma((2, max(1, depth // 1024))),
        ],
        compiler_params=pltpu.CompilerParams(vmem_limit_bytes=16 * 1024 * 1024),
    )(*held)


def solution(mesh):
    rows_v, rows_a = P(("vid", "aud"), None), P(("aud", "vid"), None)
    return jax.shard_map(
        functools.partial(on_device, mesh.shape["vid"], mesh.shape["aud"]),
        mesh=mesh,
        in_specs=(rows_v, rows_a, P(), P(), P(), P(), P(), rows_v, rows_a),
        out_specs=(rows_v, rows_a, rows_v, rows_a),
        check_vma=False,
    )
```

```python
import functools

import jax
import jax.numpy as jnp
from jax import lax
from jax.experimental import pallas as pl
from jax.experimental.pallas import tpu as pltpu
from jax.sharding import PartitionSpec as P

HS = 128
HEADS = 2
LANES = 128
MESH = pl.DeviceIdType.MESH
BF = jnp.bfloat16
F32 = jnp.float32
SCALE = float(HS) ** -0.5
SCALE2 = SCALE * 1.4426950408889634
WIDE = 3 * HS


def product(left_side, right_side, left_dim, right_dim):
    return lax.dot_general(
        left_side,
        right_side,
        (((left_dim,), (right_dim,)), ((), ())),
        preferred_element_type=F32,
    )


def head_cols(head):
    return slice(head * HS, (head + 1) * HS)


def rounded_up(value, unit):
    return (value + unit - 1) // unit * unit


def layer_kernel(
    n_vid,
    n_aud,
    video_tokens,
    audio_tokens,
    pair_weight,
    video_value,
    audio_value,
    video_output,
    audio_output,
    video_cotangent,
    audio_cotangent,
    video_rows,
    audio_fin,
    pair_w,
    value_a,
    output_a,
    rows_in,
    value_v,
    output_v,
    vown,
    aown,
    vblk,
    ablk,
    rexp,
    cexp,
    rstat,
    cstat,
    rsend,
    rrecv,
    csend,
    crecv,
    fcol,
    cfin,
    vacc,
    aacc,
    vpart,
    vrecv,
    vfar,
    apart,
    asib,
    asum,
    arecv,
    fin,
    load_sem,
    vz_send,
    vz_recv,
    vx_send,
    vx_recv,
    vr_send,
    vr_recv,
    az_send,
    az_recv,
    af_send,
    af_recv,
    rs_send,
    rs_recv,
    cs_send,
    cs_recv,
    vp_send,
    vp_recv,
    vf_send,
    vf_recv,
    as_send,
    as_recv,
    ar_send,
    ar_recv,
):
    vid, aud = lax.axis_index("vid"), lax.axis_index("aud")
    n_chip, n_pair = n_aud // 2, n_vid // 2
    core, chip = lax.rem(aud, 2), aud // 2
    head, pair = lax.rem(vid, 2), vid // 2
    other = 1 - head
    partner = 2 * pair + other
    sibling = 2 * chip + 1 - core
    tv, ta = video_tokens.shape[0], audio_tokens.shape[0]
    depth = video_tokens.shape[1]
    n_tile = n_chip // 2 * 2
    half = n_chip // 2
    rows = 2 * tv
    wide = 2 * ta
    cols = 2 * wide
    stride = rounded_up(n_tile, 8)

    def plane(dp, s):
        return 2 * lax.rem(pair + dp, n_pair) + lax.rem(head + s, 2)

    def source(dp, s):
        return 2 * lax.rem(pair + n_pair - dp, n_pair) + lax.rem(head + s, 2)

    others = [(dp, s) for dp in range(n_pair) for s in range(2) if dp or s]

    loads = []
    for i, (src, dst) in enumerate(
        (
            (pair_weight, pair_w),
            (audio_tokens, rows_in.at[1]),
            (video_tokens, rows_in.at[0]),
            (audio_value, value_a),
            (video_value, value_v),
            (audio_output, output_a),
            (audio_cotangent, rows_in.at[3]),
            (video_output, output_v),
            (video_cotangent, rows_in.at[2]),
        )
    ):
        copy = pltpu.make_async_copy(src, dst, load_sem.at[i])
        copy.start()
        loads.append(copy)

    barrier = pltpu.get_barrier_semaphore()
    count = 0
    for d in range(1, n_chip):
        pl.semaphore_signal(
            barrier,
            inc=1,
            device_id={"vid": vid, "aud": lax.rem(aud + 2 * d, n_aud)},
            device_id_type=MESH,
        )
        count += 1
    for dp, s in others:
        pl.semaphore_signal(
            barrier, inc=1, device_id={"vid": plane(dp, s), "aud": aud}, device_id_type=MESH
        )
        count += 1
    for dp in range(n_pair):
        pl.semaphore_signal(
            barrier, inc=1, device_id={"vid": plane(dp, 0), "aud": sibling}, device_id_type=MESH
        )
        count += 1

    pending = []

    def send(src, dst, send_sem, recv_sem, where):
        copy = pltpu.make_async_remote_copy(
            src_ref=src,
            dst_ref=dst,
            send_sem=send_sem,
            recv_sem=recv_sem,
            device_id={"vid": where[0], "aud": where[1]},
            device_id_type=MESH,
        )
        copy.start()
        pending.append(copy)
        return copy

    def chip_at(d):
        return (vid, lax.rem(aud + 2 * d, n_aud))

    vz, vx, vr, az, af = {}, {}, {}, {}, {}

    def put(own, k, value):
        for h in range(HEADS):
            own[h, k] = value[:, head_cols(h)].astype(BF)

    def send_near(k):
        vz[k] = send(
            vown.at[other, k], vblk.at[n_chip + chip, k], vz_send.at[k], vz_recv.at[k], (partner, aud)
        )
        for d in range(1, n_chip):
            vx[k, d] = send(
                vown.at[head, k], vblk.at[chip, k], vx_send.at[k, d], vx_recv.at[k, d], chip_at(d)
            )
        send_audio(k, 0, 1)
        af[k, 0, 0] = send(
            aown.at[head, k],
            ablk.at[pair, head, core, k],
            af_send.at[k, 0, 0],
            af_recv.at[k, 0, 0],
            (vid, sibling),
        )
        vblk[chip, k] = vown[head, k]
        ablk[pair, head, core, k] = aown[head, k]

    def send_audio(k, dp, s):
        az[k, dp, s] = send(
            aown.at[lax.rem(head + s, 2), k],
            ablk.at[pair, head, core, k],
            az_send.at[k, dp, s],
            az_recv.at[k, dp, s],
            (plane(dp, s), aud),
        )

    def relay_video(k):
        vz[k].wait_recv()
        for d in range(1, n_chip):
            vr[k, d] = send(
                vblk.at[n_chip + chip, k],
                vblk.at[n_chip + chip, k],
                vr_send.at[k, d],
                vr_recv.at[k, d],
                chip_at(d),
            )

    def relay_audio(k, dp, s):
        az[k, dp, s].wait_recv()
        z = source(dp, s)
        slot = (z // 2, lax.rem(z, 2), core, k)
        af[k, dp, s] = send(
            ablk.at[slot],
            ablk.at[slot],
            af_send.at[k, dp, s],
            af_recv.at[k, dp, s],
            (vid, sibling),
        )

    for copy in loads[:3]:
        copy.wait()
    pairs = product(rows_in[0:2].reshape(tv + ta, depth), pair_w[...], 1, 0)
    put(vown, 0, pairs[:tv])
    put(aown, 0, pairs[tv:])
    pl.semaphore_wait(barrier, count)
    send_near(0)
    for dp in range(1, n_pair):
        for s in range(2):
            send_audio(0, dp, s)
    for copy in loads[3:5]:
        copy.wait()
    put(aown, 1, product(rows_in[1], value_a[...], 1, 0))
    put(vown, 1, product(rows_in[0], value_v[...], 1, 0))
    send_near(1)
    for copy in loads[5:7]:
        copy.wait()
    put(aown, 2, product(rows_in[3], output_a[...], 1, 1))
    for copy in loads[7:9]:
        copy.wait()
    put(vown, 2, product(rows_in[2], output_v[...], 1, 1))
    send_near(2)
    for k in (1, 2):
        for dp in range(1, n_pair):
            for s in range(2):
                send_audio(k, dp, s)
    for k in range(3):
        relay_video(k)
        relay_audio(k, 0, 1)

    lane = lax.broadcasted_iota(jnp.int32, (rows, LANES), 1)

    def audio_side(dp, k):
        return ablk[lax.rem(pair + dp, n_pair), :, :, k].reshape(cols, HS)

    def video_side(tile, k):
        return vblk[pl.ds(2 * tile, 2), k].reshape(rows, HS)

    def by_eight(value):
        return value.reshape(rows // 8, 8, value.shape[-1])

    def stat_tiles(dp, role):
        def step(m, carry):
            tile = role * half + m
            scores = SCALE2 * product(video_side(tile, 0), audio_side(dp, 0), 1, 1)
            row_peak = jnp.max(scores, axis=1, keepdims=True)
            col_peak = jnp.max(by_eight(scores), axis=0)
            row_exp = jnp.exp2(scores - row_peak)
            col_exp = jnp.exp2(by_eight(scores) - col_peak[None])
            row_grad = product(video_side(tile, 2), audio_side(dp, 1), 1, 1)
            col_grad = product(video_side(tile, 1), audio_side(dp, 2), 1, 1)
            col_total = jnp.sum(col_exp, axis=0)
            col_dot = jnp.sum(col_exp * by_eight(col_grad), axis=0)
            for s in range(2):
                part = slice(s * wide, (s + 1) * wide)
                for k, value in enumerate((col_peak, col_total, col_dot)):
                    cstat[k, dp, s, tile] = value[:, part]
                rexp[dp, s, tile] = row_exp[:, part].astype(rexp.dtype)
                cexp[dp, s, tile] = (
                    col_exp[:, :, part].reshape(rows, wide).astype(cexp.dtype)
                )
            row_total = jnp.sum(row_exp, axis=1, keepdims=True)
            row_dot = jnp.sum(row_exp * row_grad, axis=1, keepdims=True)
            for k, value in enumerate((row_peak, row_total, row_dot)):
                rstat[k] = jnp.where(lane == dp * stride + tile, value, rstat[k])
            return carry

        lax.fori_loop(0, half, step, 0)

    rstat[...] = jnp.zeros_like(rstat)
    for k in range(3):
        for d in range(1, n_chip):
            vx[k, d].wait_recv()
        af[k, 0, 0].wait_recv()
        af[k, 0, 1].wait_recv()
    stat_tiles(0, 0)
    for k in range(3):
        for dp in range(1, n_pair):
            for s in range(2):
                relay_audio(k, dp, s)
    for k in range(3):
        for d in range(1, n_chip):
            vr[k, d].wait_recv()
    stat_tiles(0, 1)
    for dp in range(1, n_pair):
        for k in range(3):
            for s in range(2):
                af[k, dp, s].wait_recv()
        for role in (0, 1):
            stat_tiles(dp, role)

    def combine(parts):
        top = functools.reduce(jnp.maximum, [part[0] for part in parts])
        gains = [jnp.exp2(part[0] - top) for part in parts]
        total = sum(part[1] * gain for part, gain in zip(parts, gains))
        dots = sum(part[2] * gain for part, gain in zip(parts, gains))
        return top, total, dots

    rows_t = [rstat[k].T for k in range(3)]
    row_parts = [
        [rows_t[k][dp * stride : (dp + 1) * stride] for k in range(3)] for dp in range(n_pair)
    ]
    for k, value in enumerate(combine(row_parts)):
        rsend[k] = value
    rs = {}
    for d in range(1, n_chip):
        rs[d] = send(rsend, rrecv.at[d], rs_send.at[d], rs_recv.at[d], chip_at(d))
    for dp in range(n_pair):
        for s in range(2):
            peak = cstat[0, dp, s]
            top = jnp.max(jnp.max(peak, axis=0), axis=0, keepdims=True)
            gain = jnp.exp2(peak - top[None])
            where = (lax.rem(pair + dp, n_pair), s)
            csend[(0,) + where] = top
            for k in (1, 2):
                total = jnp.sum(cstat[k, dp, s] * gain, axis=0)
                csend[(k,) + where] = jnp.sum(total, axis=0, keepdims=True)
    cs = {}
    for dp in range(n_pair):
        for c in range(2):
            if dp or c:
                cs[dp, c] = send(
                    csend,
                    crecv.at[dp, c],
                    cs_send.at[dp, c],
                    cs_recv.at[dp, c],
                    (plane(dp, 0), sibling if c else aud),
                )
    for d in range(1, n_chip):
        rs[d].wait_recv()
    top, total, dots = combine(
        [[rsend[k] for k in range(3)]]
        + [[rrecv[d, k] for k in range(3)] for d in range(1, n_chip)]
    )
    factors = [jnp.exp2(part[0] - top) / total for part in row_parts] + [dots / total]
    blank = jnp.zeros((LANES - stride * (n_pair + 1), rows), F32)
    fcol[...] = jnp.concatenate(factors + [blank], axis=0).T
    for copy in cs.values():
        copy.wait_recv()
    col_top, col_total, col_dots = combine(
        [[csend[k] for k in range(3)]] + [[crecv[key + (k,)] for k in range(3)] for key in cs]
    )
    cfin[0] = col_top
    cfin[1] = 1.0 / col_total
    cfin[2] = col_dots / col_total

    def far_plane(dp, i):
        farthest = jnp.where(lax.rem(pair + dp, n_pair) > pair, 1, 0)
        return 1 - farthest if i else farthest

    far = [[(dp, far_plane(dp, i)) for dp in range(1, n_pair)] for i in range(2)]
    chunks = far[0] + [(0, other)] + far[1] + [(0, head)]
    n_sent = len(chunks) - 1

    def column(t):
        return jnp.sum(jnp.where(lane == t, fcol[...], 0.0), axis=1, keepdims=True)

    def tile_weights(tile, dp, s, audio):
        where = (lax.rem(pair + dp, n_pair), s)
        row_gain = column(dp * stride + tile)
        row_delta = column(n_pair * stride + tile)
        col_gain = jnp.exp2(cstat[0, dp, s, tile] - cfin[(0,) + where]) * cfin[(1,) + where]
        col_delta = cfin[(2,) + where]
        row_prob = rexp[dp, s, tile].astype(F32) * row_gain
        col_prob = (by_eight(cexp[dp, s, tile].astype(F32)) * col_gain[None]).reshape(rows, wide)
        row_grad = product(video_side(tile, 2), audio[1], 1, 1)
        col_grad = product(video_side(tile, 1), audio[2], 1, 1)
        score_grad = row_prob * (row_grad - row_delta) + col_prob * (col_grad - col_delta)
        return [value.astype(BF) for value in (row_prob, score_grad, col_prob)]

    def grad_block(tiles, indices):
        sums = [[None] * 3 for _ in tiles]
        video = [jnp.concatenate([video_side(tile, k) for tile in tiles]) for k in range(3)]
        for c in indices:
            dp, s = chunks[c]
            audio = [
                ablk[lax.rem(pair + dp, n_pair), s, :, k].reshape(wide, HS) for k in range(3)
            ]
            parts = [tile_weights(tile, dp, s, audio) for tile in tiles]
            weights = [jnp.concatenate([part[k] for part in parts]) for k in range(3)]
            for k, right in enumerate((audio[1], audio[0], audio[2])):
                value = product(weights[k], right, 1, 0)
                for i in range(len(tiles)):
                    piece = value[i * rows : (i + 1) * rows]
                    sums[i][k] = piece if sums[i][k] is None else sums[i][k] + piece
            for k, (left, right) in enumerate(((1, 2), (0, 1), (2, 0))):
                aacc[c, head_cols(k)] += product(video[left], weights[right], 0, 0)
        return sums

    def keep_sums(tile, sums):
        for k in range(3):
            vacc[tile, :, head_cols(k)] += sums[k]

    def send_sums(tile, sums):
        for k in range(3):
            total = sums[k] + vacc[tile, :, head_cols(k)]
            if k == 1:
                total = SCALE * total
            vpart[pl.ds(2 * tile, 2), :, head_cols(k)] = total.reshape(2, tv, HS).astype(BF)
        for e in range(2):
            block = 2 * tile + e
            owner = lax.rem(block, n_chip)
            slot = (block // n_chip) * n_chip + chip

            @pl.when(owner != chip)
            def _(block=block, owner=owner, slot=slot):
                pltpu.make_async_remote_copy(
                    src_ref=vpart.at[block],
                    dst_ref=vrecv.at[slot],
                    send_sem=vp_send.at[block],
                    recv_sem=vp_recv.at[slot],
                    device_id={"vid": vid, "aud": 2 * owner + core},
                    device_id_type=MESH,
                ).start()

    def tile_at(j):
        return lax.rem(j + half, n_tile)

    siblings, ar = {}, []

    def share_audio(c):
        dp, s = chunks[c]
        for j in range(2):
            for k in range(3):
                value = aacc[c, head_cols(k), j * ta : (j + 1) * ta]
                apart[dp, s, j, head_cols(k)] = (SCALE * value if k == 1 else value).astype(BF)
        siblings[c] = send(
            apart.at[dp, s, 1 - core],
            asib.at[dp, s],
            as_send.at[dp, s],
            as_recv.at[dp, s],
            (vid, sibling),
        )

    def reduce_audio(dp, s):
        both = apart[dp, s, core].astype(F32) + asib[dp, s].astype(F32)
        return both

    def send_audio_sum(dp, s):
        side = lax.rem(head + s, 2)
        asum[dp, side] = reduce_audio(dp, s).astype(BF)
        ar.append(
            send(
                asum.at[dp, side],
                arecv.at[dp, side],
                ar_send.at[dp, side],
                ar_recv.at[dp, side],
                (2 * lax.rem(pair + dp, n_pair) + s, aud),
            )
        )

    aacc[...] = jnp.zeros_like(aacc)
    vacc[...] = jnp.zeros_like(vacc)
    def leave(c):
        siblings[c].wait_recv()
        send_audio_sum(*chunks[c])

    for c in range(n_sent):
        if c < n_tile:
            tile = tile_at(c)
            send_sums(tile, grad_block([tile], range(c, len(chunks)))[0])
        if c:
            leave(c - 1)
        first = min(c + 1, n_tile)

        def step(m, carry, c=c, first=first, count=2):
            tiles = [tile_at(first + count * m + i) for i in range(count)]
            for tile, sums in zip(tiles, grad_block(tiles, [c])):
                keep_sums(tile, sums)
            return carry

        left = n_tile - first
        lax.fori_loop(0, left // 2, step, 0)
        if left % 2:
            tile = tile_at(n_tile - 1)
            keep_sums(tile, grad_block([tile], [c])[0])
        share_audio(c)

    def last_step(j, carry):
        tile = tile_at(j)
        send_sums(tile, grad_block([tile], range(n_sent, len(chunks)))[0])
        return carry

    first = min(n_sent, n_tile)
    lax.fori_loop(first, min(first + 1, n_tile), last_step, 0)
    leave(n_sent - 1)
    lax.fori_loop(min(first + 1, n_tile), n_tile, last_step, 0)
    share_audio(n_sent)

    def video_parts(role):
        for d in range(1, n_chip):
            slot = role * n_chip + lax.rem(chip + d, n_chip)
            pltpu.make_async_remote_copy(
                src_ref=vpart.at[slot],
                dst_ref=vrecv.at[slot],
                send_sem=vp_send.at[slot],
                recv_sem=vp_recv.at[slot],
                device_id={"vid": vid, "aud": chip_at(d)[1]},
                device_id_type=MESH,
            ).wait()
        total = vpart[role * n_chip + chip].astype(F32)
        for d in range(1, n_chip):
            total += vrecv[role * n_chip + lax.rem(chip + d, n_chip)].astype(F32)
        return total.astype(BF)

    vfar[0] = video_parts(1)
    relayed = send(vfar.at[0], vfar.at[1], vf_send.at[0], vf_recv.at[0], (partner, aud))
    siblings[n_sent].wait_recv()
    fin[head] = video_parts(0)
    relayed.wait_recv()
    fin[other] = vfar[1]
    for part, result, gradient in output_parts(fin, output_v, pair_w, value_v):
        video_rows[0, :, part] = result
        video_rows[1, :, part] = gradient
    mine = reduce_audio(0, head)
    for dp, side in others:
        pltpu.make_async_remote_copy(
            src_ref=asum.at[dp, side],
            dst_ref=arecv.at[dp, side],
            send_sem=ar_send.at[dp, side],
            recv_sem=ar_recv.at[dp, side],
            device_id={"vid": plane(dp, side), "aud": aud},
            device_id_type=MESH,
        ).wait_recv()
    theirs = arecv[0, 1].astype(F32)
    for dp in range(1, n_pair):
        mine += arecv[dp, 0].astype(F32)
        theirs += arecv[dp, 1].astype(F32)
    audio_fin[head] = mine.T.astype(BF)
    audio_fin[other] = theirs.T.astype(BF)
    for copy in pending:
        copy.wait_send()


def output_parts(fin, output_w, pair_w, value_w):
    mix, pairs, values = (
        jnp.concatenate([fin[h, :, head_cols(k)] for h in range(HEADS)], axis=1) for k in range(3)
    )
    depth = pair_w.shape[0]
    span = min(depth, 2048)
    for n in range(depth // span):
        part = slice(n * span, (n + 1) * span)
        yield (
            part,
            product(mix, output_w[:, part], 1, 0).astype(BF),
            (product(pairs, pair_w[part], 1, 1) + product(values, value_w[part], 1, 1)).astype(BF),
        )


def output_kernel(
    video_rows,
    audio_fin,
    pair_w,
    value_a,
    output_a,
    video_result,
    audio_result,
    video_gradient,
    audio_gradient,
    audio_rows,
    video_sem,
    audio_sem,
):
    stores = []

    def store(src, dst, sem):
        copy = pltpu.make_async_copy(src, dst, sem)
        copy.start()
        stores.append(copy)

    for i, out in enumerate((video_result, video_gradient)):
        store(video_rows.at[i], out, video_sem.at[i])
    for n, (part, *values) in enumerate(output_parts(audio_fin, output_a, pair_w, value_a)):
        for i, out in enumerate((audio_result, audio_gradient)):
            audio_rows[i, :, part] = values[i]
            store(audio_rows.at[i, :, part], out.at[:, part], audio_sem.at[i, n])
    for copy in stores:
        copy.wait()


def on_device(n_vid, n_aud, *arrays):
    tv, depth = arrays[0].shape
    ta = arrays[1].shape[0]
    hd = arrays[2].shape[1]
    n_chip, n_pair = n_aud // 2, n_vid // 2
    n_tile = n_chip
    rows, wide = 2 * tv, 2 * ta
    stride = rounded_up(n_tile, 8)
    dma = pltpu.SemaphoreType.DMA
    kept = F32 if n_pair * n_tile * rows * 2 * wide <= 2**21 else BF
    remote = [
        (3,),
        (3, n_chip),
        (3, n_chip),
        (3, n_pair, 2),
        (3, n_pair, 2),
        (n_chip,),
        (n_pair, 2),
        (2 * n_chip,),
        (1,),
        (n_pair, 2),
        (n_pair, 2),
    ]
    video_out = jax.ShapeDtypeStruct((tv, depth), BF)
    audio_out = jax.ShapeDtypeStruct((ta, depth), BF)
    vmem = pl.BlockSpec(memory_space=pltpu.VMEM)
    anywhere = pl.BlockSpec(memory_space=pl.ANY)
    held = pl.pallas_call(
        functools.partial(layer_kernel, n_vid, n_aud),
        out_shape=(
            pltpu.VMEM((2, tv, depth), BF),
            pltpu.VMEM((HEADS, ta, WIDE), BF),
            pltpu.VMEM((depth, hd), BF),
            pltpu.VMEM((depth, hd), BF),
            pltpu.VMEM((hd, depth), BF),
        ),
        in_specs=[anywhere] * 9,
        out_specs=(vmem,) * 5,
        scratch_shapes=[
            pltpu.VMEM((4, tv, depth), BF),
            pltpu.VMEM((depth, hd), BF),
            pltpu.VMEM((hd, depth), BF),
            pltpu.VMEM((HEADS, 3, tv, HS), BF),
            pltpu.VMEM((HEADS, 3, ta, HS), BF),
            pltpu.VMEM((2 * n_chip, 3, tv, HS), BF),
            pltpu.VMEM((n_pair, 2, 2, 3, ta, HS), BF),
            pltpu.VMEM((n_pair, 2, n_tile, rows, wide), kept),
            pltpu.VMEM((n_pair, 2, n_tile, rows, wide), kept),
            pltpu.VMEM((3, rows, LANES), F32),
            pltpu.VMEM((3, n_pair, 2, n_tile, 8, wide), F32),
            pltpu.VMEM((3, stride, rows), F32),
            pltpu.VMEM((n_chip, 3, stride, rows), F32),
            pltpu.VMEM((3, n_pair, 2, 1, wide), F32),
            pltpu.VMEM((n_pair, 2, 3, n_pair, 2, 1, wide), F32),
            pltpu.VMEM((rows, LANES), F32),
            pltpu.VMEM((3, n_pair, 2, 1, wide), F32),
            pltpu.VMEM((n_tile, rows, WIDE), F32),
            pltpu.VMEM((2 * n_pair, WIDE, wide), F32),
            pltpu.VMEM((2 * n_chip, tv, WIDE), BF),
            pltpu.VMEM((2 * n_chip, tv, WIDE), BF),
            pltpu.VMEM((2, tv, WIDE), BF),
            pltpu.VMEM((n_pair, 2, 2, WIDE, ta), BF),
            pltpu.VMEM((n_pair, 2, WIDE, ta), BF),
            pltpu.VMEM((n_pair, 2, WIDE, ta), BF),
            pltpu.VMEM((n_pair, 2, WIDE, ta), BF),
            pltpu.VMEM((HEADS, tv, WIDE), BF),
            dma((9,)),
        ]
        + [dma(shape) for shape in remote for _ in range(2)],
        compiler_params=pltpu.CompilerParams(
            collective_id=0, has_side_effects=True, vmem_limit_bytes=50 * 1024 * 1024
        ),
    )(*(pltpu.with_memory_space_constraint(array, pltpu.HBM) for array in arrays))
    return pl.pallas_call(
        output_kernel,
        out_shape=(video_out, audio_out, video_out, audio_out),
        in_specs=[vmem] * 5,
        out_specs=(anywhere,) * 4,
        scratch_shapes=[
            pltpu.VMEM((2, ta, depth), BF),
            dma((2,)),
            dma((2, max(1, depth // 2048))),
        ],
        compiler_params=pltpu.CompilerParams(vmem_limit_bytes=16 * 1024 * 1024),
    )(*held)


def solution(mesh):
    rows_v, rows_a = P(("vid", "aud"), None), P(("aud", "vid"), None)
    return jax.shard_map(
        functools.partial(on_device, mesh.shape["vid"], mesh.shape["aud"]),
        mesh=mesh,
        in_specs=(rows_v, rows_a, P(), P(), P(), P(), P(), rows_v, rows_a),
        out_specs=(rows_v, rows_a, rows_v, rows_a),
        check_vma=False,
    )
```

```python
import functools

import jax
import jax.numpy as jnp
from jax import lax
from jax.experimental import pallas as pl
from jax.experimental.pallas import tpu as pltpu
from jax.sharding import PartitionSpec as P

HS = 128
HEADS = 2
LANES = 128
MESH = pl.DeviceIdType.MESH
BF = jnp.bfloat16
F32 = jnp.float32
SCALE = float(HS) ** -0.5
SCALE2 = SCALE * 1.4426950408889634
WIDE = 3 * HS


def product(left_side, right_side, left_dim, right_dim):
    return lax.dot_general(
        left_side,
        right_side,
        (((left_dim,), (right_dim,)), ((), ())),
        preferred_element_type=F32,
    )


def head_cols(head):
    return slice(head * HS, (head + 1) * HS)


def rounded_up(value, unit):
    return (value + unit - 1) // unit * unit


def layer_kernel(
    n_vid,
    n_aud,
    video_tokens,
    audio_tokens,
    pair_weight,
    video_value,
    audio_value,
    video_output,
    audio_output,
    video_cotangent,
    audio_cotangent,
    audio_rows,
    video_fin,
    pair_w,
    value_v,
    output_v,
    rows_in,
    value_a,
    output_a,
    vown,
    aown,
    vblk,
    ablk,
    rexp,
    cexp,
    rstat,
    rpart,
    cstat,
    rsend,
    rrecv,
    csend,
    crecv,
    fcol,
    cfin,
    vacc,
    aacc,
    vpart,
    vrecv,
    vfar,
    apart,
    asib,
    asum,
    arecv,
    fin,
    load_sem,
    vz_send,
    vz_recv,
    vx_send,
    vx_recv,
    vr_send,
    vr_recv,
    az_send,
    az_recv,
    af_send,
    af_recv,
    rs_send,
    rs_recv,
    cs_send,
    cs_recv,
    vp_send,
    vp_recv,
    vf_send,
    vf_recv,
    as_send,
    as_recv,
    ar_send,
    ar_recv,
):
    vid, aud = lax.axis_index("vid"), lax.axis_index("aud")
    n_chip, n_pair = n_aud // 2, n_vid // 2
    core, chip = lax.rem(aud, 2), aud // 2
    head, pair = lax.rem(vid, 2), vid // 2
    other = 1 - head
    partner = 2 * pair + other
    sibling = 2 * chip + 1 - core
    tv, ta = video_tokens.shape[0], audio_tokens.shape[0]
    depth = video_tokens.shape[1]
    n_tile = n_chip // 2 * 2
    half = n_chip // 2
    rows = 2 * tv
    wide = 2 * ta
    cols = 2 * wide
    unit = rounded_up(half, 8)

    def plane(dp, s):
        return 2 * lax.rem(pair + dp, n_pair) + lax.rem(head + s, 2)

    def source(dp, s):
        return 2 * lax.rem(pair + n_pair - dp, n_pair) + lax.rem(head + s, 2)

    others = [(dp, s) for dp in range(n_pair) for s in range(2) if dp or s]

    loads = []
    for i, (src, dst) in enumerate(
        (
            (pair_weight, pair_w),
            (audio_tokens, rows_in.at[1]),
            (video_tokens, rows_in.at[0]),
            (audio_value, value_a),
            (video_value, value_v),
            (audio_output, output_a),
            (audio_cotangent, rows_in.at[3]),
            (video_output, output_v),
            (video_cotangent, rows_in.at[2]),
        )
    ):
        copy = pltpu.make_async_copy(src, dst, load_sem.at[i])
        copy.start()
        loads.append(copy)

    barrier = pltpu.get_barrier_semaphore()
    count = 0
    for d in range(1, n_chip):
        pl.semaphore_signal(
            barrier,
            inc=1,
            device_id={"vid": vid, "aud": lax.rem(aud + 2 * d, n_aud)},
            device_id_type=MESH,
        )
        count += 1
    for dp, s in others:
        pl.semaphore_signal(
            barrier, inc=1, device_id={"vid": plane(dp, s), "aud": aud}, device_id_type=MESH
        )
        count += 1
    for dp in range(n_pair):
        pl.semaphore_signal(
            barrier, inc=1, device_id={"vid": plane(dp, 0), "aud": sibling}, device_id_type=MESH
        )
        count += 1

    pending = []

    def send(src, dst, send_sem, recv_sem, where):
        copy = pltpu.make_async_remote_copy(
            src_ref=src,
            dst_ref=dst,
            send_sem=send_sem,
            recv_sem=recv_sem,
            device_id={"vid": where[0], "aud": where[1]},
            device_id_type=MESH,
        )
        copy.start()
        pending.append(copy)
        return copy

    def chip_at(d):
        return (vid, lax.rem(aud + 2 * d, n_aud))

    vz, vx, vr, az, af = {}, {}, {}, {}, {}

    def put(own, k, value):
        for h in range(HEADS):
            own[h, k] = value[:, head_cols(h)].astype(BF)

    def send_near(k):
        vz[k] = send(
            vown.at[other, k], vblk.at[n_chip + chip, k], vz_send.at[k], vz_recv.at[k], (partner, aud)
        )
        for d in range(1, n_chip):
            vx[k, d] = send(
                vown.at[head, k], vblk.at[chip, k], vx_send.at[k, d], vx_recv.at[k, d], chip_at(d)
            )
        send_audio(k, 0, 1)
        af[k, 0, 0] = send(
            aown.at[head, k],
            ablk.at[pair, head, core, k],
            af_send.at[k, 0, 0],
            af_recv.at[k, 0, 0],
            (vid, sibling),
        )
        vblk[chip, k] = vown[head, k]
        ablk[pair, head, core, k] = aown[head, k]

    def send_audio(k, dp, s):
        az[k, dp, s] = send(
            aown.at[lax.rem(head + s, 2), k],
            ablk.at[pair, head, core, k],
            az_send.at[k, dp, s],
            az_recv.at[k, dp, s],
            (plane(dp, s), aud),
        )

    def relay_video(k):
        vz[k].wait_recv()
        for d in range(1, n_chip):
            vr[k, d] = send(
                vblk.at[n_chip + chip, k],
                vblk.at[n_chip + chip, k],
                vr_send.at[k, d],
                vr_recv.at[k, d],
                chip_at(d),
            )

    def relay_audio(k, dp, s):
        az[k, dp, s].wait_recv()
        z = source(dp, s)
        slot = (z // 2, lax.rem(z, 2), core, k)
        af[k, dp, s] = send(
            ablk.at[slot],
            ablk.at[slot],
            af_send.at[k, dp, s],
            af_recv.at[k, dp, s],
            (vid, sibling),
        )

    for copy in loads[:3]:
        copy.wait()
    pairs = product(rows_in[0:2].reshape(tv + ta, depth), pair_w[...], 1, 0)
    put(vown, 0, pairs[:tv])
    put(aown, 0, pairs[tv:])
    pl.semaphore_wait(barrier, count)
    send_near(0)
    for dp in range(1, n_pair):
        for s in range(2):
            send_audio(0, dp, s)
    for copy in loads[3:5]:
        copy.wait()
    put(aown, 1, product(rows_in[1], value_a[...], 1, 0))
    put(vown, 1, product(rows_in[0], value_v[...], 1, 0))
    send_near(1)
    for copy in loads[5:7]:
        copy.wait()
    put(aown, 2, product(rows_in[3], output_a[...], 1, 1))
    for copy in loads[7:9]:
        copy.wait()
    put(vown, 2, product(rows_in[2], output_v[...], 1, 1))
    send_near(2)
    for k in (1, 2):
        for dp in range(1, n_pair):
            for s in range(2):
                send_audio(k, dp, s)
    for k in range(3):
        relay_video(k)
        relay_audio(k, 0, 1)

    lane = lax.broadcasted_iota(jnp.int32, (rows, rstat.shape[-1]), 1)

    def audio_side(dp, k):
        return ablk[lax.rem(pair + dp, n_pair), :, :, k].reshape(cols, HS)

    def video_side(tile, k):
        return vblk[pl.ds(2 * tile, 2), k].reshape(rows, HS)

    def by_eight(value):
        return value.reshape(rows // 8, 8, value.shape[-1])

    def stat_tiles(dp, role):
        def step(m, carry):
            tile = role * half + m
            scores = SCALE2 * product(video_side(tile, 0), audio_side(dp, 0), 1, 1)
            row_peak = jnp.max(scores, axis=1, keepdims=True)
            col_peak = jnp.max(by_eight(scores), axis=0)
            row_exp = jnp.exp2(scores - row_peak)
            col_exp = jnp.exp2(by_eight(scores) - col_peak[None])
            row_grad = product(video_side(tile, 2), audio_side(dp, 1), 1, 1)
            col_grad = product(video_side(tile, 1), audio_side(dp, 2), 1, 1)
            col_total = jnp.sum(col_exp, axis=0)
            col_dot = jnp.sum(col_exp * by_eight(col_grad), axis=0)
            for s in range(2):
                part = slice(s * wide, (s + 1) * wide)
                for k, value in enumerate((col_peak, col_total, col_dot)):
                    cstat[k, dp, s, tile] = value[:, part]
                rexp[dp, s, tile] = row_exp[:, part].astype(rexp.dtype)
                cexp[dp, s, tile] = (
                    col_exp[:, :, part].reshape(rows, wide).astype(cexp.dtype)
                )
            row_total = jnp.sum(row_exp, axis=1, keepdims=True)
            row_dot = jnp.sum(row_exp * row_grad, axis=1, keepdims=True)
            packed = rstat[role]
            for k, value in enumerate((row_peak, row_total, row_dot)):
                packed = jnp.where(lane == (k * n_pair + dp) * unit + m, value, packed)
            rstat[role] = packed
            return carry

        lax.fori_loop(0, half, step, 0, unroll=min(half, 2))

    def combine(parts):
        top = functools.reduce(jnp.maximum, [part[0] for part in parts])
        gains = [jnp.exp2(part[0] - top) for part in parts]
        total = sum(part[1] * gain for part, gain in zip(parts, gains))
        dots = sum(part[2] * gain for part, gain in zip(parts, gains))
        return top, total, dots

    rs, cs = {}, {}

    def row_parts(role):
        return [
            [
                rpart[role, (k * n_pair + dp) * unit : (k * n_pair + dp) * unit + half]
                for k in range(3)
            ]
            for dp in range(n_pair)
        ]

    def share_rows(role):
        rpart[role] = rstat[role].T
        for k, value in enumerate(combine(row_parts(role))):
            rsend[role, k * half : (k + 1) * half] = value
        for d in range(1, n_chip):
            rs[role, d] = send(
                rsend.at[role],
                rrecv.at[role, d],
                rs_send.at[role, d],
                rs_recv.at[role, d],
                chip_at(d),
            )

    def finish_rows(role):
        for d in range(1, n_chip):
            rs[role, d].wait_recv()
        top, total, dots = combine(
            [[rsend[role, k * half : (k + 1) * half] for k in range(3)]]
            + [
                [rrecv[role, d, k * half : (k + 1) * half] for k in range(3)]
                for d in range(1, n_chip)
            ]
        )
        inverse = 1.0 / total
        factors = [jnp.exp2(part[0] - top) * inverse for part in row_parts(role)]
        factors.append(dots * inverse)
        for i, value in enumerate(factors):
            rpart[role, i * unit : i * unit + half] = value
        fcol[role] = rpart[role].T

    def share_columns(dp):
        where = lax.rem(pair + dp, n_pair)
        for s in range(2):
            peak = cstat[0, dp, s]
            top = jnp.max(jnp.max(peak, axis=0), axis=0, keepdims=True)
            gain = jnp.exp2(peak - top[None])
            csend[where, s : s + 1] = top
            for k in (1, 2):
                total = jnp.sum(cstat[k, dp, s] * gain, axis=0)
                row = 2 * k + s
                csend[where, row : row + 1] = jnp.sum(total, axis=0, keepdims=True)
        for dq in reversed(range(n_pair)):
            for c in range(2):
                if dq or c:
                    cs[dp, dq, c] = send(
                        csend.at[where],
                        crecv.at[dq, c, where],
                        cs_send.at[where, dq, c],
                        cs_recv.at[where, dq, c],
                        (plane(dq, 0), sibling if c else aud),
                    )

    def finish_columns(dp):
        where = lax.rem(pair + dp, n_pair)
        pieces = [slice(2 * k, 2 * k + 2) for k in range(3)]
        parts = [[csend[where, piece] for piece in pieces]]
        for key, copy in cs.items():
            if key[0] == dp:
                copy.wait_recv()
                parts.append([crecv[key[1:] + (where, piece)] for piece in pieces])
        top, total, dots = combine(parts)
        inverse = 1.0 / total
        for k, value in enumerate((top, inverse, dots * inverse)):
            for s in range(2):
                cfin[k, where, s] = value[s : s + 1]

    for ref in (rstat, rsend, csend):
        ref[...] = jnp.zeros_like(ref)
    for k in range(3):
        for d in range(1, n_chip):
            vx[k, d].wait_recv()
        af[k, 0, 0].wait_recv()
        af[k, 0, 1].wait_recv()
    stat_tiles(0, 0)
    for k in range(3):
        for dp in range(1, n_pair):
            for s in range(2):
                relay_audio(k, dp, s)
    for k in range(3):
        for d in range(1, n_chip):
            vr[k, d].wait_recv()
    stat_tiles(0, 1)
    share_columns(0)
    for dp in range(1, n_pair):
        for k in range(3):
            for s in range(2):
                af[k, dp, s].wait_recv()
        stat_tiles(dp, 1)
        if dp == n_pair - 1:
            share_rows(1)
        stat_tiles(dp, 0)
        share_columns(dp)
    if n_pair == 1:
        share_rows(1)
    share_rows(0)
    finish_rows(1)
    for dp in range(n_pair):
        finish_columns(dp)

    def far_plane(dp, i):
        farthest = jnp.where(lax.rem(pair + dp, n_pair) > pair, 1, 0)
        return 1 - farthest if i else farthest

    far = [[(dp, far_plane(dp, i)) for dp in range(1, n_pair)] for i in range(2)]
    chunks = far[0] + [(0, other)] + far[1] + [(0, head)]
    n_sent = len(chunks) - 1

    def column(role, t):
        return jnp.sum(jnp.where(lane == t, fcol[role], 0.0), axis=1, keepdims=True)

    def tile_weights(tile, dp, s, audio):
        where = (lax.rem(pair + dp, n_pair), s)
        role, m = tile // half, lax.rem(tile, half)
        row_gain = column(role, dp * unit + m)
        row_delta = column(role, n_pair * unit + m)
        col_gain = jnp.exp2(cstat[0, dp, s, tile] - cfin[(0,) + where]) * cfin[(1,) + where]
        col_delta = cfin[(2,) + where]
        row_prob = rexp[dp, s, tile].astype(F32) * row_gain
        col_prob = (by_eight(cexp[dp, s, tile].astype(F32)) * col_gain[None]).reshape(rows, wide)
        row_grad = product(video_side(tile, 2), audio[1], 1, 1)
        col_grad = product(video_side(tile, 1), audio[2], 1, 1)
        score_grad = row_prob * (row_grad - row_delta) + col_prob * (col_grad - col_delta)
        return [value.astype(BF) for value in (row_prob, score_grad, col_prob)]

    def grad_block(tiles, indices):
        sums = [[None] * 3 for _ in tiles]
        video = [jnp.concatenate([video_side(tile, k) for tile in tiles]) for k in range(3)]
        for c in indices:
            dp, s = chunks[c]
            audio = [
                ablk[lax.rem(pair + dp, n_pair), s, :, k].reshape(wide, HS) for k in range(3)
            ]
            parts = [tile_weights(tile, dp, s, audio) for tile in tiles]
            weights = [jnp.concatenate([part[k] for part in parts]) for k in range(3)]
            for k, right in enumerate((audio[1], audio[0], audio[2])):
                value = product(weights[k], right, 1, 0)
                for i in range(len(tiles)):
                    piece = value[i * rows : (i + 1) * rows]
                    sums[i][k] = piece if sums[i][k] is None else sums[i][k] + piece
            for k, (left, right) in enumerate(((1, 2), (0, 1), (2, 0))):
                aacc[c, head_cols(k)] += product(video[left], weights[right], 0, 0)
        return sums

    def keep_sums(tile, sums):
        for k in range(3):
            vacc[tile, :, head_cols(k)] += sums[k]

    def send_sums(tile, sums):
        for k in range(3):
            total = sums[k] + vacc[tile, :, head_cols(k)]
            if k == 1:
                total = SCALE * total
            vpart[pl.ds(2 * tile, 2), :, head_cols(k)] = total.reshape(2, tv, HS).astype(BF)
        for e in range(2):
            block = 2 * tile + e
            owner = lax.rem(block, n_chip)
            slot = (block // n_chip) * n_chip + chip

            @pl.when(owner != chip)
            def _(block=block, owner=owner, slot=slot):
                pltpu.make_async_remote_copy(
                    src_ref=vpart.at[block],
                    dst_ref=vrecv.at[slot],
                    send_sem=vp_send.at[block],
                    recv_sem=vp_recv.at[slot],
                    device_id={"vid": vid, "aud": 2 * owner + core},
                    device_id_type=MESH,
                ).start()

    def tile_at(j):
        return lax.rem(j + half, n_tile)

    siblings, ar = {}, []

    def share_audio(c):
        dp, s = chunks[c]
        for j in range(2):
            for k in range(3):
                value = aacc[c, head_cols(k), j * ta : (j + 1) * ta]
                apart[dp, s, j, head_cols(k)] = (SCALE * value if k == 1 else value).astype(BF)
        siblings[c] = send(
            apart.at[dp, s, 1 - core],
            asib.at[dp, s],
            as_send.at[dp, s],
            as_recv.at[dp, s],
            (vid, sibling),
        )

    def reduce_audio(dp, s):
        both = apart[dp, s, core].astype(F32) + asib[dp, s].astype(F32)
        return both

    def send_audio_sum(dp, s):
        side = lax.rem(head + s, 2)
        asum[dp, side] = reduce_audio(dp, s).astype(BF)
        ar.append(
            send(
                asum.at[dp, side],
                arecv.at[dp, side],
                ar_send.at[dp, side],
                ar_recv.at[dp, side],
                (2 * lax.rem(pair + dp, n_pair) + s, aud),
            )
        )

    aacc[...] = jnp.zeros_like(aacc)
    vacc[...] = jnp.zeros_like(vacc)
    def leave(c):
        siblings[c].wait_recv()
        send_audio_sum(*chunks[c])

    for c in range(n_sent):
        if c < n_tile:
            tile = tile_at(c)
            send_sums(tile, grad_block([tile], range(c, len(chunks)))[0])
        if c:
            leave(c - 1)
        else:
            finish_rows(0)
        first = min(c + 1, n_tile)

        def step(m, carry, c=c, first=first, count=2):
            tiles = [tile_at(first + count * m + i) for i in range(count)]
            for tile, sums in zip(tiles, grad_block(tiles, [c])):
                keep_sums(tile, sums)
            return carry

        left = n_tile - first
        lax.fori_loop(0, left // 2, step, 0)
        if left % 2:
            tile = tile_at(n_tile - 1)
            keep_sums(tile, grad_block([tile], [c])[0])
        share_audio(c)

    def last_step(j, carry):
        tile = tile_at(j)
        send_sums(tile, grad_block([tile], range(n_sent, len(chunks)))[0])
        return carry

    first = min(n_sent, n_tile)
    lax.fori_loop(first, min(first + 1, n_tile), last_step, 0)
    leave(n_sent - 1)
    lax.fori_loop(min(first + 1, n_tile), n_tile, last_step, 0)
    share_audio(n_sent)

    def video_parts(role):
        for d in range(1, n_chip):
            slot = role * n_chip + lax.rem(chip + d, n_chip)
            pltpu.make_async_remote_copy(
                src_ref=vpart.at[slot],
                dst_ref=vrecv.at[slot],
                send_sem=vp_send.at[slot],
                recv_sem=vp_recv.at[slot],
                device_id={"vid": vid, "aud": chip_at(d)[1]},
                device_id_type=MESH,
            ).wait()
        total = vpart[role * n_chip + chip].astype(F32)
        for d in range(1, n_chip):
            total += vrecv[role * n_chip + lax.rem(chip + d, n_chip)].astype(F32)
        return total.astype(BF)

    vfar[0] = video_parts(1)
    relayed = send(vfar.at[0], vfar.at[1], vf_send.at[0], vf_recv.at[0], (partner, aud))
    siblings[n_sent].wait_recv()
    mine = reduce_audio(0, head)
    for dp, side in others:
        pltpu.make_async_remote_copy(
            src_ref=asum.at[dp, side],
            dst_ref=arecv.at[dp, side],
            send_sem=ar_send.at[dp, side],
            recv_sem=ar_recv.at[dp, side],
            device_id={"vid": plane(dp, side), "aud": aud},
            device_id_type=MESH,
        ).wait_recv()
    theirs = arecv[0, 1].astype(F32)
    for dp in range(1, n_pair):
        mine += arecv[dp, 0].astype(F32)
        theirs += arecv[dp, 1].astype(F32)
    fin[head] = mine.T.astype(BF)
    fin[other] = theirs.T.astype(BF)
    for part, result, gradient in output_parts(fin, output_a, pair_w, value_a):
        audio_rows[0, :, part] = result
        audio_rows[1, :, part] = gradient
    video_fin[head] = video_parts(0)
    relayed.wait_recv()
    video_fin[other] = vfar[1]
    for copy in pending:
        copy.wait_send()


def output_parts(fin, output_w, pair_w, value_w):
    mix, pairs, values = (
        jnp.concatenate([fin[h, :, head_cols(k)] for h in range(HEADS)], axis=1) for k in range(3)
    )
    depth = pair_w.shape[0]
    span = min(depth, 2048)
    for n in range(depth // span):
        part = slice(n * span, (n + 1) * span)
        yield (
            part,
            product(mix, output_w[:, part], 1, 0).astype(BF),
            (product(pairs, pair_w[part], 1, 1) + product(values, value_w[part], 1, 1)).astype(BF),
        )


def output_kernel(
    audio_rows,
    video_fin,
    pair_w,
    value_v,
    output_v,
    video_result,
    audio_result,
    video_gradient,
    audio_gradient,
    video_rows,
    audio_sem,
    video_sem,
):
    stores = []

    def store(src, dst, sem):
        copy = pltpu.make_async_copy(src, dst, sem)
        copy.start()
        stores.append(copy)

    for i, out in enumerate((audio_result, audio_gradient)):
        store(audio_rows.at[i], out, audio_sem.at[i])
    for n, (part, *values) in enumerate(output_parts(video_fin, output_v, pair_w, value_v)):
        for i, out in enumerate((video_result, video_gradient)):
            video_rows[i, :, part] = values[i]
            store(video_rows.at[i, :, part], out.at[:, part], video_sem.at[i, n])
    for copy in stores:
        copy.wait()


def on_device(n_vid, n_aud, *arrays):
    tv, depth = arrays[0].shape
    ta = arrays[1].shape[0]
    hd = arrays[2].shape[1]
    n_chip, n_pair = n_aud // 2, n_vid // 2
    n_tile = n_chip
    rows, wide = 2 * tv, 2 * ta
    unit = rounded_up(n_chip // 2, 8)
    lanes = rounded_up(3 * n_pair * unit, LANES)
    dma = pltpu.SemaphoreType.DMA
    kept = F32 if n_pair * n_tile * rows * 2 * wide <= 2**21 else BF
    remote = [
        (3,),
        (3, n_chip),
        (3, n_chip),
        (3, n_pair, 2),
        (3, n_pair, 2),
        (2, n_chip),
        (n_pair, n_pair, 2),
        (2 * n_chip,),
        (1,),
        (n_pair, 2),
        (n_pair, 2),
    ]
    video_out = jax.ShapeDtypeStruct((tv, depth), BF)
    audio_out = jax.ShapeDtypeStruct((ta, depth), BF)
    vmem = pl.BlockSpec(memory_space=pltpu.VMEM)
    anywhere = pl.BlockSpec(memory_space=pl.ANY)
    held = pl.pallas_call(
        functools.partial(layer_kernel, n_vid, n_aud),
        out_shape=(
            pltpu.VMEM((2, ta, depth), BF),
            pltpu.VMEM((HEADS, tv, WIDE), BF),
            pltpu.VMEM((depth, hd), BF),
            pltpu.VMEM((depth, hd), BF),
            pltpu.VMEM((hd, depth), BF),
        ),
        in_specs=[anywhere] * 9,
        out_specs=(vmem,) * 5,
        scratch_shapes=[
            pltpu.VMEM((4, tv, depth), BF),
            pltpu.VMEM((depth, hd), BF),
            pltpu.VMEM((hd, depth), BF),
            pltpu.VMEM((HEADS, 3, tv, HS), BF),
            pltpu.VMEM((HEADS, 3, ta, HS), BF),
            pltpu.VMEM((2 * n_chip, 3, tv, HS), BF),
            pltpu.VMEM((n_pair, 2, 2, 3, ta, HS), BF),
            pltpu.VMEM((n_pair, 2, n_tile, rows, wide), kept),
            pltpu.VMEM((n_pair, 2, n_tile, rows, wide), kept),
            pltpu.VMEM((2, rows, lanes), F32),
            pltpu.VMEM((2, lanes, rows), F32),
            pltpu.VMEM((3, n_pair, 2, n_tile, 8, wide), F32),
            pltpu.VMEM((2, rounded_up(3 * n_chip // 2, 8), rows), F32),
            pltpu.VMEM((2, n_chip, rounded_up(3 * n_chip // 2, 8), rows), F32),
            pltpu.VMEM((n_pair, 8, wide), F32),
            pltpu.VMEM((n_pair, 2, n_pair, 8, wide), F32),
            pltpu.VMEM((2, rows, lanes), F32),
            pltpu.VMEM((3, n_pair, 2, 1, wide), F32),
            pltpu.VMEM((n_tile, rows, WIDE), F32),
            pltpu.VMEM((2 * n_pair, WIDE, wide), F32),
            pltpu.VMEM((2 * n_chip, tv, WIDE), BF),
            pltpu.VMEM((2 * n_chip, tv, WIDE), BF),
            pltpu.VMEM((2, tv, WIDE), BF),
            pltpu.VMEM((n_pair, 2, 2, WIDE, ta), BF),
            pltpu.VMEM((n_pair, 2, WIDE, ta), BF),
            pltpu.VMEM((n_pair, 2, WIDE, ta), BF),
            pltpu.VMEM((n_pair, 2, WIDE, ta), BF),
            pltpu.VMEM((HEADS, ta, WIDE), BF),
            dma((9,)),
        ]
        + [dma(shape) for shape in remote for _ in range(2)],
        compiler_params=pltpu.CompilerParams(
            collective_id=0, has_side_effects=True, vmem_limit_bytes=50 * 1024 * 1024
        ),
    )(*(pltpu.with_memory_space_constraint(array, pltpu.HBM) for array in arrays))
    return pl.pallas_call(
        output_kernel,
        out_shape=(video_out, audio_out, video_out, audio_out),
        in_specs=[vmem] * 5,
        out_specs=(anywhere,) * 4,
        scratch_shapes=[
            pltpu.VMEM((2, tv, depth), BF),
            dma((2,)),
            dma((2, max(1, depth // 2048))),
        ],
        compiler_params=pltpu.CompilerParams(vmem_limit_bytes=16 * 1024 * 1024),
    )(*held)


def solution(mesh):
    rows_v, rows_a = P(("vid", "aud"), None), P(("aud", "vid"), None)
    return jax.shard_map(
        functools.partial(on_device, mesh.shape["vid"], mesh.shape["aud"]),
        mesh=mesh,
        in_specs=(rows_v, rows_a, P(), P(), P(), P(), P(), rows_v, rows_a),
        out_specs=(rows_v, rows_a, rows_v, rows_a),
        check_vma=False,
    )
```

```python
import functools

import jax
import jax.numpy as jnp
from jax import lax
from jax.experimental import pallas as pl
from jax.experimental.pallas import tpu as pltpu
from jax.sharding import PartitionSpec as P

HS = 128
HEADS = 2
LANES = 128
MESH = pl.DeviceIdType.MESH
BF = jnp.bfloat16
F32 = jnp.float32
SCALE = float(HS) ** -0.5
SCALE2 = SCALE * 1.4426950408889634
WIDE = 3 * HS


def product(left_side, right_side, left_dim, right_dim):
    return lax.dot_general(
        left_side,
        right_side,
        (((left_dim,), (right_dim,)), ((), ())),
        preferred_element_type=F32,
    )


def head_cols(head):
    return slice(head * HS, (head + 1) * HS)


def rounded_up(value, unit):
    return (value + unit - 1) // unit * unit


def layer_kernel(
    n_vid,
    n_aud,
    video_tokens,
    audio_tokens,
    pair_weight,
    video_value,
    audio_value,
    video_output,
    audio_output,
    video_cotangent,
    audio_cotangent,
    audio_rows,
    video_fin,
    pair_w,
    value_v,
    output_v,
    rows_in,
    value_a,
    output_a,
    vown,
    aown,
    vblk,
    ablk,
    rexp,
    cexp,
    rstat,
    rpart,
    cstat,
    rsend,
    rrecv,
    csend,
    crecv,
    fcol,
    cfin,
    vacc,
    aacc,
    vpart,
    vrecv,
    vfar,
    apart,
    asib,
    asum,
    arecv,
    fin,
    load_sem,
    vz_send,
    vz_recv,
    vx_send,
    vx_recv,
    vr_send,
    vr_recv,
    az_send,
    az_recv,
    af_send,
    af_recv,
    rs_send,
    rs_recv,
    cs_send,
    cs_recv,
    vp_send,
    vp_recv,
    vf_send,
    vf_recv,
    as_send,
    as_recv,
    ar_send,
    ar_recv,
):
    vid, aud = lax.axis_index("vid"), lax.axis_index("aud")
    n_chip, n_pair = n_aud // 2, n_vid // 2
    core, chip = lax.rem(aud, 2), aud // 2
    head, pair = lax.rem(vid, 2), vid // 2
    other = 1 - head
    partner = 2 * pair + other
    sibling = 2 * chip + 1 - core
    tv, ta = video_tokens.shape[0], audio_tokens.shape[0]
    depth = video_tokens.shape[1]
    n_tile = n_chip // 2 * 2
    half = n_chip // 2
    rows = 2 * tv
    wide = 2 * ta
    cols = 2 * wide
    unit = rounded_up(half, 8)

    def plane(dp, s):
        return 2 * lax.rem(pair + dp, n_pair) + lax.rem(head + s, 2)

    def source(dp, s):
        return 2 * lax.rem(pair + n_pair - dp, n_pair) + lax.rem(head + s, 2)

    others = [(dp, s) for dp in range(n_pair) for s in range(2) if dp or s]

    loads = []
    for i, (src, dst) in enumerate(
        (
            (pair_weight, pair_w),
            (audio_tokens, rows_in.at[1]),
            (video_tokens, rows_in.at[0]),
            (audio_value, value_a),
            (video_value, value_v),
            (audio_output, output_a),
            (audio_cotangent, rows_in.at[3]),
            (video_output, output_v),
            (video_cotangent, rows_in.at[2]),
        )
    ):
        copy = pltpu.make_async_copy(src, dst, load_sem.at[i])
        copy.start()
        loads.append(copy)

    barrier = pltpu.get_barrier_semaphore()
    count = 0
    for d in range(1, n_chip):
        pl.semaphore_signal(
            barrier,
            inc=1,
            device_id={"vid": vid, "aud": lax.rem(aud + 2 * d, n_aud)},
            device_id_type=MESH,
        )
        count += 1
    for dp, s in others:
        pl.semaphore_signal(
            barrier, inc=1, device_id={"vid": plane(dp, s), "aud": aud}, device_id_type=MESH
        )
        count += 1
    for dp in range(n_pair):
        pl.semaphore_signal(
            barrier, inc=1, device_id={"vid": plane(dp, 0), "aud": sibling}, device_id_type=MESH
        )
        count += 1

    pending = []

    def send(src, dst, send_sem, recv_sem, where):
        copy = pltpu.make_async_remote_copy(
            src_ref=src,
            dst_ref=dst,
            send_sem=send_sem,
            recv_sem=recv_sem,
            device_id={"vid": where[0], "aud": where[1]},
            device_id_type=MESH,
        )
        copy.start()
        pending.append(copy)
        return copy

    def chip_at(d):
        return (vid, lax.rem(aud + 2 * d, n_aud))

    vz, vx, vr, az, af = {}, {}, {}, {}, {}

    def put(own, k, value):
        for h in range(HEADS):
            own[h, k] = value[:, head_cols(h)].astype(BF)

    def send_near(k):
        vz[k] = send(
            vown.at[other, k], vblk.at[n_chip + chip, k], vz_send.at[k], vz_recv.at[k], (partner, aud)
        )
        for d in range(1, n_chip):
            vx[k, d] = send(
                vown.at[head, k], vblk.at[chip, k], vx_send.at[k, d], vx_recv.at[k, d], chip_at(d)
            )
        send_audio(k, 0, 1)
        af[k, 0, 0] = send(
            aown.at[head, k],
            ablk.at[pair, head, core, k],
            af_send.at[k, 0, 0],
            af_recv.at[k, 0, 0],
            (vid, sibling),
        )
        vblk[chip, k] = vown[head, k]
        ablk[pair, head, core, k] = aown[head, k]

    def send_audio(k, dp, s):
        az[k, dp, s] = send(
            aown.at[lax.rem(head + s, 2), k],
            ablk.at[pair, head, core, k],
            az_send.at[k, dp, s],
            az_recv.at[k, dp, s],
            (plane(dp, s), aud),
        )

    def relay_video(k):
        vz[k].wait_recv()
        for d in range(1, n_chip):
            vr[k, d] = send(
                vblk.at[n_chip + chip, k],
                vblk.at[n_chip + chip, k],
                vr_send.at[k, d],
                vr_recv.at[k, d],
                chip_at(d),
            )

    def relay_audio(k, dp, s):
        az[k, dp, s].wait_recv()
        z = source(dp, s)
        slot = (z // 2, lax.rem(z, 2), core, k)
        af[k, dp, s] = send(
            ablk.at[slot],
            ablk.at[slot],
            af_send.at[k, dp, s],
            af_recv.at[k, dp, s],
            (vid, sibling),
        )

    for copy in loads[:3]:
        copy.wait()
    pairs = product(rows_in[0:2].reshape(tv + ta, depth), pair_w[...], 1, 0)
    put(vown, 0, pairs[:tv])
    put(aown, 0, pairs[tv:])
    pl.semaphore_wait(barrier, count)
    send_near(0)
    for dp in range(1, n_pair):
        for s in range(2):
            send_audio(0, dp, s)
    for copy in loads[3:5]:
        copy.wait()
    put(aown, 1, product(rows_in[1], value_a[...], 1, 0))
    put(vown, 1, product(rows_in[0], value_v[...], 1, 0))
    send_near(1)
    for copy in loads[5:7]:
        copy.wait()
    put(aown, 2, product(rows_in[3], output_a[...], 1, 1))
    for copy in loads[7:9]:
        copy.wait()
    put(vown, 2, product(rows_in[2], output_v[...], 1, 1))
    send_near(2)
    for k in (1, 2):
        for dp in range(1, n_pair):
            for s in range(2):
                send_audio(k, dp, s)
    for k in range(3):
        relay_video(k)
        relay_audio(k, 0, 1)

    lane = lax.broadcasted_iota(jnp.int32, (rows, rstat.shape[-1]), 1)

    def audio_side(dp, k):
        return ablk[lax.rem(pair + dp, n_pair), :, :, k].reshape(cols, HS)

    def video_side(tile, k):
        return vblk[pl.ds(2 * tile, 2), k].reshape(rows, HS)

    def by_eight(value):
        return value.reshape(rows // 8, 8, value.shape[-1])

    def stat_tiles(dp, role):
        def step(m, carry):
            tile = role * half + m
            scores = SCALE2 * product(video_side(tile, 0), audio_side(dp, 0), 1, 1)
            row_peak = jnp.max(scores, axis=1, keepdims=True)
            col_peak = jnp.max(by_eight(scores), axis=0)
            row_exp = jnp.exp2(scores - row_peak)
            col_exp = jnp.exp2(by_eight(scores) - col_peak[None])
            row_grad = product(video_side(tile, 2), audio_side(dp, 1), 1, 1)
            col_grad = product(video_side(tile, 1), audio_side(dp, 2), 1, 1)
            col_total = jnp.sum(col_exp, axis=0)
            col_dot = jnp.sum(col_exp * by_eight(col_grad), axis=0)
            for s in range(2):
                part = slice(s * wide, (s + 1) * wide)
                for k, value in enumerate((col_peak, col_total, col_dot)):
                    cstat[k, dp, s, tile] = value[:, part]
                rexp[dp, s, tile] = row_exp[:, part].astype(rexp.dtype)
                cexp[dp, s, tile] = (
                    col_exp[:, :, part].reshape(rows, wide).astype(cexp.dtype)
                )
            row_total = jnp.sum(row_exp, axis=1, keepdims=True)
            row_dot = jnp.sum(row_exp * row_grad, axis=1, keepdims=True)
            packed = rstat[role]
            for k, value in enumerate((row_peak, row_total, row_dot)):
                packed = jnp.where(lane == (k * n_pair + dp) * unit + m, value, packed)
            rstat[role] = packed
            return carry

        lax.fori_loop(0, half, step, 0, unroll=min(half, 2))

    def combine(parts):
        top = functools.reduce(jnp.maximum, [part[0] for part in parts])
        gains = [jnp.exp2(part[0] - top) for part in parts]
        total = sum(part[1] * gain for part, gain in zip(parts, gains))
        dots = sum(part[2] * gain for part, gain in zip(parts, gains))
        return top, total, dots

    rs, cs = {}, {}

    def row_parts(role):
        return [
            [
                rpart[role, (k * n_pair + dp) * unit : (k * n_pair + dp) * unit + half]
                for k in range(3)
            ]
            for dp in range(n_pair)
        ]

    def share_rows(role):
        rpart[role] = rstat[role].T
        for k, value in enumerate(combine(row_parts(role))):
            rsend[role, k * half : (k + 1) * half] = value
        for d in range(1, n_chip):
            rs[role, d] = send(
                rsend.at[role],
                rrecv.at[role, d],
                rs_send.at[role, d],
                rs_recv.at[role, d],
                chip_at(d),
            )

    def finish_rows(role):
        for d in range(1, n_chip):
            rs[role, d].wait_recv()
        top, total, dots = combine(
            [[rsend[role, k * half : (k + 1) * half] for k in range(3)]]
            + [
                [rrecv[role, d, k * half : (k + 1) * half] for k in range(3)]
                for d in range(1, n_chip)
            ]
        )
        inverse = 1.0 / total
        factors = [jnp.exp2(part[0] - top) * inverse for part in row_parts(role)]
        factors.append(dots * inverse)
        for i, value in enumerate(factors):
            rpart[role, i * unit : i * unit + half] = value
        fcol[role] = rpart[role].T

    def share_columns(dp):
        where = lax.rem(pair + dp, n_pair)
        for s in range(2):
            peak = cstat[0, dp, s]
            top = jnp.max(jnp.max(peak, axis=0), axis=0, keepdims=True)
            gain = jnp.exp2(peak - top[None])
            csend[where, s : s + 1] = top
            for k in (1, 2):
                total = jnp.sum(cstat[k, dp, s] * gain, axis=0)
                row = 2 * k + s
                csend[where, row : row + 1] = jnp.sum(total, axis=0, keepdims=True)
        for dq in reversed(range(n_pair)):
            for c in range(2):
                if dq or c:
                    cs[dp, dq, c] = send(
                        csend.at[where],
                        crecv.at[dq, c, where],
                        cs_send.at[where, dq, c],
                        cs_recv.at[where, dq, c],
                        (plane(dq, 0), sibling if c else aud),
                    )

    def finish_columns(dp):
        where = lax.rem(pair + dp, n_pair)
        pieces = [slice(2 * k, 2 * k + 2) for k in range(3)]
        parts = [[csend[where, piece] for piece in pieces]]
        for key, copy in cs.items():
            if key[0] == dp:
                copy.wait_recv()
                parts.append([crecv[key[1:] + (where, piece)] for piece in pieces])
        top, total, dots = combine(parts)
        inverse = 1.0 / total
        for k, value in enumerate((top, inverse, dots * inverse)):
            for s in range(2):
                cfin[k, where, s] = value[s : s + 1]

    for ref in (rstat, rsend, csend, aacc, vacc):
        ref[...] = jnp.zeros_like(ref)
    for k in range(3):
        for d in range(1, n_chip):
            vx[k, d].wait_recv()
        af[k, 0, 0].wait_recv()
        af[k, 0, 1].wait_recv()
    stat_tiles(0, 0)
    for k in range(3):
        for dp in range(1, n_pair):
            for s in range(2):
                relay_audio(k, dp, s)
    for k in range(3):
        for d in range(1, n_chip):
            vr[k, d].wait_recv()
    stat_tiles(0, 1)
    share_columns(0)
    for dp in range(1, n_pair):
        for k in range(3):
            for s in range(2):
                af[k, dp, s].wait_recv()
        stat_tiles(dp, 1)
        if dp == n_pair - 1:
            share_rows(1)
        stat_tiles(dp, 0)
        share_columns(dp)
    if n_pair == 1:
        share_rows(1)
    share_rows(0)
    finish_rows(1)
    for dp in range(n_pair):
        finish_columns(dp)

    def far_plane(dp, i):
        farthest = jnp.where(lax.rem(pair + dp, n_pair) > pair, 1, 0)
        return 1 - farthest if i else farthest

    far = [[(dp, far_plane(dp, i)) for dp in range(1, n_pair)] for i in range(2)]
    chunks = far[0] + [(0, other)] + far[1] + [(0, head)]
    n_sent = len(chunks) - 1

    def column(role, t):
        return jnp.sum(jnp.where(lane == t, fcol[role], 0.0), axis=1, keepdims=True)

    def tile_weights(tile, dp, s, audio, row_gain, row_delta):
        where = (lax.rem(pair + dp, n_pair), s)
        col_gain = jnp.exp2(cstat[0, dp, s, tile] - cfin[(0,) + where]) * cfin[(1,) + where]
        col_delta = cfin[(2,) + where]
        row_prob = rexp[dp, s, tile].astype(F32) * row_gain
        col_prob = (by_eight(cexp[dp, s, tile].astype(F32)) * col_gain[None]).reshape(rows, wide)
        row_grad = product(video_side(tile, 2), audio[1], 1, 1)
        col_grad = product(video_side(tile, 1), audio[2], 1, 1)
        score_grad = row_prob * (row_grad - row_delta) + col_prob * (col_grad - col_delta)
        return [value.astype(BF) for value in (row_prob, score_grad, col_prob)]

    def grad_block(tiles, indices):
        sums = [[None] * 3 for _ in tiles]
        known = {}
        video = [jnp.concatenate([video_side(tile, k) for tile in tiles]) for k in range(3)]
        for c in indices:
            dp, s = chunks[c]
            audio = [
                ablk[lax.rem(pair + dp, n_pair), s, :, k].reshape(wide, HS) for k in range(3)
            ]
            parts = []
            for i, tile in enumerate(tiles):
                role, m = tile // half, lax.rem(tile, half)
                for index in (dp, n_pair):
                    if (i, index) not in known:
                        known[i, index] = column(role, index * unit + m)
                parts.append(
                    tile_weights(tile, dp, s, audio, known[i, dp], known[i, n_pair])
                )
            weights = [jnp.concatenate([part[k] for part in parts]) for k in range(3)]
            for k, right in enumerate((audio[1], audio[0], audio[2])):
                value = product(weights[k], right, 1, 0)
                for i in range(len(tiles)):
                    piece = value[i * rows : (i + 1) * rows]
                    sums[i][k] = piece if sums[i][k] is None else sums[i][k] + piece
            for k, (left, right) in enumerate(((1, 2), (0, 1), (2, 0))):
                aacc[c, head_cols(k)] += product(video[left], weights[right], 0, 0)
        return sums

    def keep_sums(tile, sums):
        for k in range(3):
            vacc[tile, :, head_cols(k)] += sums[k]

    def send_sums(tile, sums):
        for k in range(3):
            total = sums[k] + vacc[tile, :, head_cols(k)]
            if k == 1:
                total = SCALE * total
            vpart[pl.ds(2 * tile, 2), :, head_cols(k)] = total.reshape(2, tv, HS).astype(BF)
        for e in range(2):
            block = 2 * tile + e
            owner = lax.rem(block, n_chip)
            slot = (block // n_chip) * n_chip + chip

            @pl.when(owner != chip)
            def _(block=block, owner=owner, slot=slot):
                pltpu.make_async_remote_copy(
                    src_ref=vpart.at[block],
                    dst_ref=vrecv.at[slot],
                    send_sem=vp_send.at[block],
                    recv_sem=vp_recv.at[slot],
                    device_id={"vid": vid, "aud": 2 * owner + core},
                    device_id_type=MESH,
                ).start()

    def tile_at(j):
        return lax.rem(j + half, n_tile)

    siblings, ar = {}, []

    def share_audio(c):
        dp, s = chunks[c]
        for j in range(2):
            for k in range(3):
                value = aacc[c, head_cols(k), j * ta : (j + 1) * ta]
                apart[dp, s, j, head_cols(k)] = (SCALE * value if k == 1 else value).astype(BF)
        siblings[c] = send(
            apart.at[dp, s, 1 - core],
            asib.at[dp, s],
            as_send.at[dp, s],
            as_recv.at[dp, s],
            (vid, sibling),
        )

    def reduce_audio(dp, s):
        both = apart[dp, s, core].astype(F32) + asib[dp, s].astype(F32)
        return both

    def send_audio_sum(dp, s):
        side = lax.rem(head + s, 2)
        asum[dp, side] = reduce_audio(dp, s).astype(BF)
        ar.append(
            send(
                asum.at[dp, side],
                arecv.at[dp, side],
                ar_send.at[dp, side],
                ar_recv.at[dp, side],
                (2 * lax.rem(pair + dp, n_pair) + s, aud),
            )
        )

    def leave(c):
        siblings[c].wait_recv()
        send_audio_sum(*chunks[c])

    for c in range(n_sent):
        if c < n_tile:
            tile = tile_at(c)
            send_sums(tile, grad_block([tile], range(c, len(chunks)))[0])
        if c:
            leave(c - 1)
        else:
            finish_rows(0)
        first = min(c + 1, n_tile)

        def step(m, carry, c=c, first=first, count=2):
            tiles = [tile_at(first + count * m + i) for i in range(count)]
            for tile, sums in zip(tiles, grad_block(tiles, [c])):
                keep_sums(tile, sums)
            return carry

        left = n_tile - first
        lax.fori_loop(0, left // 2, step, 0)
        if left % 2:
            tile = tile_at(n_tile - 1)
            keep_sums(tile, grad_block([tile], [c])[0])
        share_audio(c)

    def last_step(j, carry):
        tile = tile_at(j)
        send_sums(tile, grad_block([tile], range(n_sent, len(chunks)))[0])
        return carry

    first = min(n_sent, n_tile)
    lax.fori_loop(first, min(first + 1, n_tile), last_step, 0)
    leave(n_sent - 1)
    lax.fori_loop(min(first + 1, n_tile), n_tile, last_step, 0)
    share_audio(n_sent)

    def video_parts(role):
        for d in range(1, n_chip):
            slot = role * n_chip + lax.rem(chip + d, n_chip)
            pltpu.make_async_remote_copy(
                src_ref=vpart.at[slot],
                dst_ref=vrecv.at[slot],
                send_sem=vp_send.at[slot],
                recv_sem=vp_recv.at[slot],
                device_id={"vid": vid, "aud": chip_at(d)[1]},
                device_id_type=MESH,
            ).wait()
        total = vpart[role * n_chip + chip].astype(F32)
        for d in range(1, n_chip):
            total += vrecv[role * n_chip + lax.rem(chip + d, n_chip)].astype(F32)
        return total.astype(BF)

    vfar[0] = video_parts(1)
    relayed = send(vfar.at[0], vfar.at[1], vf_send.at[0], vf_recv.at[0], (partner, aud))
    siblings[n_sent].wait_recv()
    mine = reduce_audio(0, head)
    for dp, side in others:
        pltpu.make_async_remote_copy(
            src_ref=asum.at[dp, side],
            dst_ref=arecv.at[dp, side],
            send_sem=ar_send.at[dp, side],
            recv_sem=ar_recv.at[dp, side],
            device_id={"vid": plane(dp, side), "aud": aud},
            device_id_type=MESH,
        ).wait_recv()
    theirs = arecv[0, 1].astype(F32)
    for dp in range(1, n_pair):
        mine += arecv[dp, 0].astype(F32)
        theirs += arecv[dp, 1].astype(F32)
    fin[head] = mine.T.astype(BF)
    fin[other] = theirs.T.astype(BF)
    for part, result, gradient in output_parts(fin, output_a, pair_w, value_a):
        audio_rows[0, :, part] = result
        audio_rows[1, :, part] = gradient
    video_fin[head] = video_parts(0)
    relayed.wait_recv()
    video_fin[other] = vfar[1]
    for copy in pending:
        copy.wait_send()


def output_parts(fin, output_w, pair_w, value_w):
    mix, pairs, values = (
        jnp.concatenate([fin[h, :, head_cols(k)] for h in range(HEADS)], axis=1) for k in range(3)
    )
    depth = pair_w.shape[0]
    edges = (0, depth // 2, depth * 7 // 8, depth)
    for first, last in zip(edges, edges[1:]):
        part = slice(first, last)
        yield (
            part,
            product(mix, output_w[:, part], 1, 0).astype(BF),
            (product(pairs, pair_w[part], 1, 1) + product(values, value_w[part], 1, 1)).astype(BF),
        )


def output_kernel(
    audio_rows,
    video_fin,
    pair_w,
    value_v,
    output_v,
    video_result,
    audio_result,
    video_gradient,
    audio_gradient,
    video_rows,
    audio_sem,
    video_sem,
):
    stores = []

    def store(src, dst, sem):
        copy = pltpu.make_async_copy(src, dst, sem)
        copy.start()
        stores.append(copy)

    for i, out in enumerate((audio_result, audio_gradient)):
        store(audio_rows.at[i], out, audio_sem.at[i])
    for n, (part, *values) in enumerate(output_parts(video_fin, output_v, pair_w, value_v)):
        for i, out in enumerate((video_result, video_gradient)):
            video_rows[i, :, part] = values[i]
            store(video_rows.at[i, :, part], out.at[:, part], video_sem.at[i, n])
    for copy in stores:
        copy.wait()


def on_device(n_vid, n_aud, *arrays):
    tv, depth = arrays[0].shape
    ta = arrays[1].shape[0]
    hd = arrays[2].shape[1]
    n_chip, n_pair = n_aud // 2, n_vid // 2
    n_tile = n_chip
    rows, wide = 2 * tv, 2 * ta
    unit = rounded_up(n_chip // 2, 8)
    lanes = rounded_up(3 * n_pair * unit, LANES)
    dma = pltpu.SemaphoreType.DMA
    kept = F32 if n_pair * n_tile * rows * 2 * wide <= 2**21 else BF
    remote = [
        (3,),
        (3, n_chip),
        (3, n_chip),
        (3, n_pair, 2),
        (3, n_pair, 2),
        (2, n_chip),
        (n_pair, n_pair, 2),
        (2 * n_chip,),
        (1,),
        (n_pair, 2),
        (n_pair, 2),
    ]
    video_out = jax.ShapeDtypeStruct((tv, depth), BF)
    audio_out = jax.ShapeDtypeStruct((ta, depth), BF)
    vmem = pl.BlockSpec(memory_space=pltpu.VMEM)
    anywhere = pl.BlockSpec(memory_space=pl.ANY)
    held = pl.pallas_call(
        functools.partial(layer_kernel, n_vid, n_aud),
        out_shape=(
            pltpu.VMEM((2, ta, depth), BF),
            pltpu.VMEM((HEADS, tv, WIDE), BF),
            pltpu.VMEM((depth, hd), BF),
            pltpu.VMEM((depth, hd), BF),
            pltpu.VMEM((hd, depth), BF),
        ),
        in_specs=[anywhere] * 9,
        out_specs=(vmem,) * 5,
        scratch_shapes=[
            pltpu.VMEM((4, tv, depth), BF),
            pltpu.VMEM((depth, hd), BF),
            pltpu.VMEM((hd, depth), BF),
            pltpu.VMEM((HEADS, 3, tv, HS), BF),
            pltpu.VMEM((HEADS, 3, ta, HS), BF),
            pltpu.VMEM((2 * n_chip, 3, tv, HS), BF),
            pltpu.VMEM((n_pair, 2, 2, 3, ta, HS), BF),
            pltpu.VMEM((n_pair, 2, n_tile, rows, wide), kept),
            pltpu.VMEM((n_pair, 2, n_tile, rows, wide), kept),
            pltpu.VMEM((2, rows, lanes), F32),
            pltpu.VMEM((2, lanes, rows), F32),
            pltpu.VMEM((3, n_pair, 2, n_tile, 8, wide), F32),
            pltpu.VMEM((2, rounded_up(3 * n_chip // 2, 8), rows), F32),
            pltpu.VMEM((2, n_chip, rounded_up(3 * n_chip // 2, 8), rows), F32),
            pltpu.VMEM((n_pair, 8, wide), F32),
            pltpu.VMEM((n_pair, 2, n_pair, 8, wide), F32),
            pltpu.VMEM((2, rows, lanes), F32),
            pltpu.VMEM((3, n_pair, 2, 1, wide), F32),
            pltpu.VMEM((n_tile, rows, WIDE), F32),
            pltpu.VMEM((2 * n_pair, WIDE, wide), F32),
            pltpu.VMEM((2 * n_chip, tv, WIDE), BF),
            pltpu.VMEM((2 * n_chip, tv, WIDE), BF),
            pltpu.VMEM((2, tv, WIDE), BF),
            pltpu.VMEM((n_pair, 2, 2, WIDE, ta), BF),
            pltpu.VMEM((n_pair, 2, WIDE, ta), BF),
            pltpu.VMEM((n_pair, 2, WIDE, ta), BF),
            pltpu.VMEM((n_pair, 2, WIDE, ta), BF),
            pltpu.VMEM((HEADS, ta, WIDE), BF),
            dma((9,)),
        ]
        + [dma(shape) for shape in remote for _ in range(2)],
        compiler_params=pltpu.CompilerParams(
            collective_id=0, has_side_effects=True, vmem_limit_bytes=50 * 1024 * 1024
        ),
    )(*(pltpu.with_memory_space_constraint(array, pltpu.HBM) for array in arrays))
    return pl.pallas_call(
        output_kernel,
        out_shape=(video_out, audio_out, video_out, audio_out),
        in_specs=[vmem] * 5,
        out_specs=(anywhere,) * 4,
        scratch_shapes=[
            pltpu.VMEM((2, tv, depth), BF),
            dma((2,)),
            dma((2, 3)),
        ],
        compiler_params=pltpu.CompilerParams(vmem_limit_bytes=16 * 1024 * 1024),
    )(*held)


def solution(mesh):
    rows_v, rows_a = P(("vid", "aud"), None), P(("aud", "vid"), None)
    return jax.shard_map(
        functools.partial(on_device, mesh.shape["vid"], mesh.shape["aud"]),
        mesh=mesh,
        in_specs=(rows_v, rows_a, P(), P(), P(), P(), P(), rows_v, rows_a),
        out_specs=(rows_v, rows_a, rows_v, rows_a),
        check_vma=False,
    )
```

```python
import functools

import jax
import jax.numpy as jnp
from jax import lax
from jax.experimental import pallas as pl
from jax.experimental.pallas import tpu as pltpu
from jax.sharding import PartitionSpec as P

HS = 128
HEADS = 2
LANES = 128
MESH = pl.DeviceIdType.MESH
BF = jnp.bfloat16
F32 = jnp.float32
SCALE = float(HS) ** -0.5
SCALE2 = SCALE * 1.4426950408889634
WIDE = 3 * HS


def product(left_side, right_side, left_dim, right_dim):
    return lax.dot_general(
        left_side,
        right_side,
        (((left_dim,), (right_dim,)), ((), ())),
        preferred_element_type=F32,
    )


def head_cols(head):
    return slice(head * HS, (head + 1) * HS)


def rounded_up(value, unit):
    return (value + unit - 1) // unit * unit


def layer_kernel(
    n_vid,
    n_aud,
    video_tokens,
    audio_tokens,
    pair_weight,
    video_value,
    audio_value,
    video_output,
    audio_output,
    video_cotangent,
    audio_cotangent,
    audio_rows,
    video_fin,
    pair_w,
    value_v,
    output_v,
    rows_in,
    value_a,
    output_a,
    vown,
    aown,
    vblk,
    ablk,
    rexp,
    cexp,
    rstat,
    rpart,
    cstat,
    rsend,
    rrecv,
    csend,
    crecv,
    fcol,
    cfin,
    vacc,
    aacc,
    vpart,
    vrecv,
    vfar,
    apart,
    asib,
    asum,
    arecv,
    fin,
    load_sem,
    vz_send,
    vz_recv,
    vx_send,
    vx_recv,
    vr_send,
    vr_recv,
    az_send,
    az_recv,
    af_send,
    af_recv,
    rs_send,
    rs_recv,
    cs_send,
    cs_recv,
    vp_send,
    vp_recv,
    vf_send,
    vf_recv,
    as_send,
    as_recv,
    ar_send,
    ar_recv,
):
    vid, aud = lax.axis_index("vid"), lax.axis_index("aud")
    n_chip, n_pair = n_aud // 2, n_vid // 2
    core, chip = lax.rem(aud, 2), aud // 2
    head, pair = lax.rem(vid, 2), vid // 2
    other = 1 - head
    partner = 2 * pair + other
    sibling = 2 * chip + 1 - core
    tv, ta = video_tokens.shape[0], audio_tokens.shape[0]
    depth = video_tokens.shape[1]
    n_tile = n_chip // 2 * 2
    half = n_chip // 2
    rows = 2 * tv
    wide = 2 * ta
    cols = 2 * wide
    unit = rounded_up(half, 8)

    def plane(dp, s):
        return 2 * lax.rem(pair + dp, n_pair) + lax.rem(head + s, 2)

    def source(dp, s):
        return 2 * lax.rem(pair + n_pair - dp, n_pair) + lax.rem(head + s, 2)

    others = [(dp, s) for dp in range(n_pair) for s in range(2) if dp or s]

    loads = []
    for i, (src, dst) in enumerate(
        (
            (pair_weight, pair_w),
            (audio_tokens, rows_in.at[1]),
            (video_tokens, rows_in.at[0]),
            (audio_value, value_a),
            (video_value, value_v),
            (audio_output, output_a),
            (audio_cotangent, rows_in.at[3]),
            (video_output, output_v),
            (video_cotangent, rows_in.at[2]),
        )
    ):
        copy = pltpu.make_async_copy(src, dst, load_sem.at[i])
        copy.start()
        loads.append(copy)

    barrier = pltpu.get_barrier_semaphore()
    count = 0
    for d in range(1, n_chip):
        pl.semaphore_signal(
            barrier,
            inc=1,
            device_id={"vid": vid, "aud": lax.rem(aud + 2 * d, n_aud)},
            device_id_type=MESH,
        )
        count += 1
    for dp, s in others:
        pl.semaphore_signal(
            barrier, inc=1, device_id={"vid": plane(dp, s), "aud": aud}, device_id_type=MESH
        )
        count += 1
    for dp in range(n_pair):
        pl.semaphore_signal(
            barrier, inc=1, device_id={"vid": plane(dp, 0), "aud": sibling}, device_id_type=MESH
        )
        count += 1

    pending = []

    def send(src, dst, send_sem, recv_sem, where):
        copy = pltpu.make_async_remote_copy(
            src_ref=src,
            dst_ref=dst,
            send_sem=send_sem,
            recv_sem=recv_sem,
            device_id={"vid": where[0], "aud": where[1]},
            device_id_type=MESH,
        )
        copy.start()
        pending.append(copy)
        return copy

    def chip_at(d):
        return (vid, lax.rem(aud + 2 * d, n_aud))

    vz, vx, vr, az, af = {}, {}, {}, {}, {}

    def put(own, k, value):
        for h in range(HEADS):
            own[h, k] = value[:, head_cols(h)].astype(BF)

    def send_near(k):
        vz[k] = send(
            vown.at[other, k], vblk.at[n_chip + chip, k], vz_send.at[k], vz_recv.at[k], (partner, aud)
        )
        for d in range(1, n_chip):
            vx[k, d] = send(
                vown.at[head, k], vblk.at[chip, k], vx_send.at[k, d], vx_recv.at[k, d], chip_at(d)
            )
        send_audio(k, 0, 1)
        af[k, 0, 0] = send(
            aown.at[head, k],
            ablk.at[pair, head, core, k],
            af_send.at[k, 0, 0],
            af_recv.at[k, 0, 0],
            (vid, sibling),
        )
        vblk[chip, k] = vown[head, k]
        ablk[pair, head, core, k] = aown[head, k]

    def send_audio(k, dp, s):
        az[k, dp, s] = send(
            aown.at[lax.rem(head + s, 2), k],
            ablk.at[pair, head, core, k],
            az_send.at[k, dp, s],
            az_recv.at[k, dp, s],
            (plane(dp, s), aud),
        )

    def relay_video(k):
        vz[k].wait_recv()
        for d in range(1, n_chip):
            vr[k, d] = send(
                vblk.at[n_chip + chip, k],
                vblk.at[n_chip + chip, k],
                vr_send.at[k, d],
                vr_recv.at[k, d],
                chip_at(d),
            )

    def relay_audio(k, dp, s):
        az[k, dp, s].wait_recv()
        z = source(dp, s)
        slot = (z // 2, lax.rem(z, 2), core, k)
        af[k, dp, s] = send(
            ablk.at[slot],
            ablk.at[slot],
            af_send.at[k, dp, s],
            af_recv.at[k, dp, s],
            (vid, sibling),
        )

    for copy in loads[:3]:
        copy.wait()
    pairs = product(rows_in[0:2].reshape(tv + ta, depth), pair_w[...], 1, 0)
    put(vown, 0, pairs[:tv])
    put(aown, 0, pairs[tv:])
    pl.semaphore_wait(barrier, count)
    send_near(0)
    for dp in range(1, n_pair):
        for s in range(2):
            send_audio(0, dp, s)
    for copy in loads[3:5]:
        copy.wait()
    put(aown, 1, product(rows_in[1], value_a[...], 1, 0))
    put(vown, 1, product(rows_in[0], value_v[...], 1, 0))
    send_near(1)
    for copy in loads[5:7]:
        copy.wait()
    put(aown, 2, product(rows_in[3], output_a[...], 1, 1))
    for copy in loads[7:9]:
        copy.wait()
    put(vown, 2, product(rows_in[2], output_v[...], 1, 1))
    send_near(2)
    for k in (1, 2):
        for dp in range(1, n_pair):
            for s in range(2):
                send_audio(k, dp, s)
    for k in range(3):
        relay_video(k)
        relay_audio(k, 0, 1)
    for dp in range(1, n_pair):
        for s in range(2):
            relay_audio(0, dp, s)

    lane = lax.broadcasted_iota(jnp.int32, (rows, rstat.shape[-1]), 1)

    def audio_side(dp, k):
        return ablk[lax.rem(pair + dp, n_pair), :, :, k].reshape(cols, HS)

    def video_side(tile, k):
        return vblk[pl.ds(2 * tile, 2), k].reshape(rows, HS)

    def by_eight(value):
        return value.reshape(rows // 8, 8, value.shape[-1])

    def stat_tiles(dp, role):
        def step(m, carry):
            tile = role * half + m
            scores = SCALE2 * product(video_side(tile, 0), audio_side(dp, 0), 1, 1)
            row_peak = jnp.max(scores, axis=1, keepdims=True)
            col_peak = jnp.max(by_eight(scores), axis=0)
            row_exp = jnp.exp2(scores - row_peak)
            col_exp = jnp.exp2(by_eight(scores) - col_peak[None])
            row_grad = product(video_side(tile, 2), audio_side(dp, 1), 1, 1)
            col_grad = product(video_side(tile, 1), audio_side(dp, 2), 1, 1)
            col_total = jnp.sum(col_exp, axis=0)
            col_dot = jnp.sum(col_exp * by_eight(col_grad), axis=0)
            for s in range(2):
                part = slice(s * wide, (s + 1) * wide)
                for k, value in enumerate((col_peak, col_total, col_dot)):
                    cstat[k, dp, s, tile] = value[:, part]
                rexp[dp, s, tile] = row_exp[:, part].astype(rexp.dtype)
                cexp[dp, s, tile] = (
                    col_exp[:, :, part].reshape(rows, wide).astype(cexp.dtype)
                )
            row_total = jnp.sum(row_exp, axis=1, keepdims=True)
            row_dot = jnp.sum(row_exp * row_grad, axis=1, keepdims=True)
            packed = rstat[role]
            for k, value in enumerate((row_peak, row_total, row_dot)):
                packed = jnp.where(lane == (k * n_pair + dp) * unit + m, value, packed)
            rstat[role] = packed
            return carry

        lax.fori_loop(0, half, step, 0, unroll=min(half, 2))

    def combine(parts):
        top = functools.reduce(jnp.maximum, [part[0] for part in parts])
        gains = [jnp.exp2(part[0] - top) for part in parts]
        total = sum(part[1] * gain for part, gain in zip(parts, gains))
        dots = sum(part[2] * gain for part, gain in zip(parts, gains))
        return top, total, dots

    rs, cs = {}, {}

    def row_parts(role):
        return [
            [
                rpart[role, (k * n_pair + dp) * unit : (k * n_pair + dp) * unit + half]
                for k in range(3)
            ]
            for dp in range(n_pair)
        ]

    def share_rows(role):
        rpart[role] = rstat[role].T
        for k, value in enumerate(combine(row_parts(role))):
            rsend[role, k * half : (k + 1) * half] = value
        for d in range(1, n_chip):
            rs[role, d] = send(
                rsend.at[role],
                rrecv.at[role, d],
                rs_send.at[role, d],
                rs_recv.at[role, d],
                chip_at(d),
            )

    def finish_rows(role):
        for d in range(1, n_chip):
            rs[role, d].wait_recv()
        top, total, dots = combine(
            [[rsend[role, k * half : (k + 1) * half] for k in range(3)]]
            + [
                [rrecv[role, d, k * half : (k + 1) * half] for k in range(3)]
                for d in range(1, n_chip)
            ]
        )
        inverse = 1.0 / total
        factors = [jnp.exp2(part[0] - top) * inverse for part in row_parts(role)]
        factors.append(dots * inverse)
        for i, value in enumerate(factors):
            rpart[role, i * unit : i * unit + half] = value
        fcol[role] = rpart[role].T

    def share_columns(dp):
        where = lax.rem(pair + dp, n_pair)
        for s in range(2):
            peak = cstat[0, dp, s]
            top = jnp.max(jnp.max(peak, axis=0), axis=0, keepdims=True)
            gain = jnp.exp2(peak - top[None])
            csend[where, s : s + 1] = top
            for k in (1, 2):
                total = jnp.sum(cstat[k, dp, s] * gain, axis=0)
                row = 2 * k + s
                csend[where, row : row + 1] = jnp.sum(total, axis=0, keepdims=True)
        for dq in reversed(range(n_pair)):
            for c in range(2):
                if dq or c:
                    cs[dp, dq, c] = send(
                        csend.at[where],
                        crecv.at[dq, c, where],
                        cs_send.at[where, dq, c],
                        cs_recv.at[where, dq, c],
                        (plane(dq, 0), sibling if c else aud),
                    )

    def finish_columns(dp):
        where = lax.rem(pair + dp, n_pair)
        pieces = [slice(2 * k, 2 * k + 2) for k in range(3)]
        parts = [[csend[where, piece] for piece in pieces]]
        for key, copy in cs.items():
            if key[0] == dp:
                copy.wait_recv()
                parts.append([crecv[key[1:] + (where, piece)] for piece in pieces])
        top, total, dots = combine(parts)
        inverse = 1.0 / total
        for k, value in enumerate((top, inverse, dots * inverse)):
            for s in range(2):
                cfin[k, where, s] = value[s : s + 1]

    for ref in (rstat, rsend, csend, aacc, vacc):
        ref[...] = jnp.zeros_like(ref)
    for k in range(3):
        for d in range(1, n_chip):
            vx[k, d].wait_recv()
        af[k, 0, 0].wait_recv()
        af[k, 0, 1].wait_recv()
    stat_tiles(0, 0)
    for k in (1, 2):
        for dp in range(1, n_pair):
            for s in range(2):
                relay_audio(k, dp, s)
    for k in range(3):
        for d in range(1, n_chip):
            vr[k, d].wait_recv()
    stat_tiles(0, 1)
    share_columns(0)
    for dp in range(1, n_pair):
        for k in range(3):
            for s in range(2):
                af[k, dp, s].wait_recv()
        stat_tiles(dp, 1)
        if dp == n_pair - 1:
            share_rows(1)
        stat_tiles(dp, 0)
        share_columns(dp)
    if n_pair == 1:
        share_rows(1)
    share_rows(0)
    finish_rows(1)
    for dp in range(n_pair):
        finish_columns(dp)

    def far_plane(dp, i):
        farthest = jnp.where(lax.rem(pair + dp, n_pair) > pair, 1, 0)
        return 1 - farthest if i else farthest

    far = [[(dp, far_plane(dp, i)) for dp in range(1, n_pair)] for i in range(2)]
    chunks = far[0] + [(0, other)] + far[1] + [(0, head)]
    n_sent = len(chunks) - 1

    def column(role, t):
        return jnp.sum(jnp.where(lane == t, fcol[role], 0.0), axis=1, keepdims=True)

    def tile_weights(tile, dp, s, audio, row_gain, row_delta):
        where = (lax.rem(pair + dp, n_pair), s)
        col_gain = jnp.exp2(cstat[0, dp, s, tile] - cfin[(0,) + where]) * cfin[(1,) + where]
        col_delta = cfin[(2,) + where]
        row_prob = rexp[dp, s, tile].astype(F32) * row_gain
        col_prob = (by_eight(cexp[dp, s, tile].astype(F32)) * col_gain[None]).reshape(rows, wide)
        row_grad = product(video_side(tile, 2), audio[1], 1, 1)
        col_grad = product(video_side(tile, 1), audio[2], 1, 1)
        score_grad = row_prob * (row_grad - row_delta) + col_prob * (col_grad - col_delta)
        return [value.astype(BF) for value in (row_prob, score_grad, col_prob)]

    def grad_block(tiles, indices):
        sums = [[None] * 3 for _ in tiles]
        known = {}
        video = [jnp.concatenate([video_side(tile, k) for tile in tiles]) for k in range(3)]
        for c in indices:
            dp, s = chunks[c]
            audio = [
                ablk[lax.rem(pair + dp, n_pair), s, :, k].reshape(wide, HS) for k in range(3)
            ]
            parts = []
            for i, tile in enumerate(tiles):
                role, m = tile // half, lax.rem(tile, half)
                for index in (dp, n_pair):
                    if (i, index) not in known:
                        known[i, index] = column(role, index * unit + m)
                parts.append(
                    tile_weights(tile, dp, s, audio, known[i, dp], known[i, n_pair])
                )
            weights = [jnp.concatenate([part[k] for part in parts]) for k in range(3)]
            for k, right in enumerate((audio[1], audio[0], audio[2])):
                value = product(weights[k], right, 1, 0)
                for i in range(len(tiles)):
                    piece = value[i * rows : (i + 1) * rows]
                    sums[i][k] = piece if sums[i][k] is None else sums[i][k] + piece
            for k, (left, right) in enumerate(((1, 2), (0, 1), (2, 0))):
                aacc[c, head_cols(k)] += product(video[left], weights[right], 0, 0)
        return sums

    def keep_sums(tile, sums):
        for k in range(3):
            vacc[tile, :, head_cols(k)] += sums[k]

    def send_sums(tile, sums):
        for k in range(3):
            total = sums[k] + vacc[tile, :, head_cols(k)]
            if k == 1:
                total = SCALE * total
            vpart[pl.ds(2 * tile, 2), :, head_cols(k)] = total.reshape(2, tv, HS).astype(BF)
        for e in range(2):
            block = 2 * tile + e
            owner = lax.rem(block, n_chip)
            slot = (block // n_chip) * n_chip + chip

            @pl.when(owner != chip)
            def _(block=block, owner=owner, slot=slot):
                pltpu.make_async_remote_copy(
                    src_ref=vpart.at[block],
                    dst_ref=vrecv.at[slot],
                    send_sem=vp_send.at[block],
                    recv_sem=vp_recv.at[slot],
                    device_id={"vid": vid, "aud": 2 * owner + core},
                    device_id_type=MESH,
                ).start()

    def tile_at(j):
        return lax.rem(j + half, n_tile)

    siblings, ar = {}, []

    def share_audio(c):
        dp, s = chunks[c]
        for j in range(2):
            for k in range(3):
                value = aacc[c, head_cols(k), j * ta : (j + 1) * ta]
                apart[dp, s, j, head_cols(k)] = (SCALE * value if k == 1 else value).astype(BF)
        siblings[c] = send(
            apart.at[dp, s, 1 - core],
            asib.at[dp, s],
            as_send.at[dp, s],
            as_recv.at[dp, s],
            (vid, sibling),
        )

    def reduce_audio(dp, s):
        both = apart[dp, s, core].astype(F32) + asib[dp, s].astype(F32)
        return both

    def send_audio_sum(dp, s):
        side = lax.rem(head + s, 2)
        asum[dp, side] = reduce_audio(dp, s).astype(BF)
        ar.append(
            send(
                asum.at[dp, side],
                arecv.at[dp, side],
                ar_send.at[dp, side],
                ar_recv.at[dp, side],
                (2 * lax.rem(pair + dp, n_pair) + s, aud),
            )
        )

    def leave(c):
        siblings[c].wait_recv()
        send_audio_sum(*chunks[c])

    for c in range(n_sent):
        if c < n_tile:
            tile = tile_at(c)
            send_sums(tile, grad_block([tile], range(c, len(chunks)))[0])
        if c:
            leave(c - 1)
        else:
            finish_rows(0)
        first = min(c + 1, n_tile)

        def step(m, carry, c=c, first=first, count=2):
            tiles = [tile_at(first + count * m + i) for i in range(count)]
            for tile, sums in zip(tiles, grad_block(tiles, [c])):
                keep_sums(tile, sums)
            return carry

        left = n_tile - first
        lax.fori_loop(0, left // 2, step, 0)
        if left % 2:
            tile = tile_at(n_tile - 1)
            keep_sums(tile, grad_block([tile], [c])[0])
        share_audio(c)

    def last_step(j, carry):
        tile = tile_at(j)
        send_sums(tile, grad_block([tile], range(n_sent, len(chunks)))[0])
        return carry

    first = min(n_sent, n_tile)
    lax.fori_loop(first, min(first + 1, n_tile), last_step, 0)
    leave(n_sent - 1)
    lax.fori_loop(min(first + 1, n_tile), n_tile, last_step, 0)
    share_audio(n_sent)

    def video_parts(role):
        for d in range(1, n_chip):
            slot = role * n_chip + lax.rem(chip + d, n_chip)
            pltpu.make_async_remote_copy(
                src_ref=vpart.at[slot],
                dst_ref=vrecv.at[slot],
                send_sem=vp_send.at[slot],
                recv_sem=vp_recv.at[slot],
                device_id={"vid": vid, "aud": chip_at(d)[1]},
                device_id_type=MESH,
            ).wait()
        total = vpart[role * n_chip + chip].astype(F32)
        for d in range(1, n_chip):
            total += vrecv[role * n_chip + lax.rem(chip + d, n_chip)].astype(F32)
        return total.astype(BF)

    vfar[0] = video_parts(1)
    relayed = send(vfar.at[0], vfar.at[1], vf_send.at[0], vf_recv.at[0], (partner, aud))
    siblings[n_sent].wait_recv()
    mine = reduce_audio(0, head)
    for dp, side in others:
        pltpu.make_async_remote_copy(
            src_ref=asum.at[dp, side],
            dst_ref=arecv.at[dp, side],
            send_sem=ar_send.at[dp, side],
            recv_sem=ar_recv.at[dp, side],
            device_id={"vid": plane(dp, side), "aud": aud},
            device_id_type=MESH,
        ).wait_recv()
    theirs = arecv[0, 1].astype(F32)
    for dp in range(1, n_pair):
        mine += arecv[dp, 0].astype(F32)
        theirs += arecv[dp, 1].astype(F32)
    fin[head] = mine.T.astype(BF)
    fin[other] = theirs.T.astype(BF)
    for part, result, gradient in output_parts(fin, output_a, pair_w, value_a):
        audio_rows[0, :, part] = result
        audio_rows[1, :, part] = gradient
    video_fin[head] = video_parts(0)
    relayed.wait_recv()
    video_fin[other] = vfar[1]
    for copy in pending:
        copy.wait_send()


def output_parts(fin, output_w, pair_w, value_w):
    mix, pairs, values = (
        jnp.concatenate([fin[h, :, head_cols(k)] for h in range(HEADS)], axis=1) for k in range(3)
    )
    depth = pair_w.shape[0]
    edges = (0, depth // 2, depth * 7 // 8, depth)
    for first, last in zip(edges, edges[1:]):
        part = slice(first, last)
        yield (
            part,
            product(mix, output_w[:, part], 1, 0).astype(BF),
            (product(pairs, pair_w[part], 1, 1) + product(values, value_w[part], 1, 1)).astype(BF),
        )


def output_kernel(
    audio_rows,
    video_fin,
    pair_w,
    value_v,
    output_v,
    video_result,
    audio_result,
    video_gradient,
    audio_gradient,
    video_rows,
    audio_sem,
    video_sem,
):
    stores = []

    def store(src, dst, sem):
        copy = pltpu.make_async_copy(src, dst, sem)
        copy.start()
        stores.append(copy)

    for i, out in enumerate((audio_result, audio_gradient)):
        store(audio_rows.at[i], out, audio_sem.at[i])
    for n, (part, *values) in enumerate(output_parts(video_fin, output_v, pair_w, value_v)):
        for i, out in enumerate((video_result, video_gradient)):
            video_rows[i, :, part] = values[i]
            store(video_rows.at[i, :, part], out.at[:, part], video_sem.at[i, n])
    for copy in stores:
        copy.wait()


def on_device(n_vid, n_aud, *arrays):
    tv, depth = arrays[0].shape
    ta = arrays[1].shape[0]
    hd = arrays[2].shape[1]
    n_chip, n_pair = n_aud // 2, n_vid // 2
    n_tile = n_chip
    rows, wide = 2 * tv, 2 * ta
    unit = rounded_up(n_chip // 2, 8)
    lanes = rounded_up(3 * n_pair * unit, LANES)
    dma = pltpu.SemaphoreType.DMA
    kept = F32 if n_pair * n_tile * rows * 2 * wide <= 2**21 else BF
    remote = [
        (3,),
        (3, n_chip),
        (3, n_chip),
        (3, n_pair, 2),
        (3, n_pair, 2),
        (2, n_chip),
        (n_pair, n_pair, 2),
        (2 * n_chip,),
        (1,),
        (n_pair, 2),
        (n_pair, 2),
    ]
    video_out = jax.ShapeDtypeStruct((tv, depth), BF)
    audio_out = jax.ShapeDtypeStruct((ta, depth), BF)
    vmem = pl.BlockSpec(memory_space=pltpu.VMEM)
    anywhere = pl.BlockSpec(memory_space=pl.ANY)
    held = pl.pallas_call(
        functools.partial(layer_kernel, n_vid, n_aud),
        out_shape=(
            pltpu.VMEM((2, ta, depth), BF),
            pltpu.VMEM((HEADS, tv, WIDE), BF),
            pltpu.VMEM((depth, hd), BF),
            pltpu.VMEM((depth, hd), BF),
            pltpu.VMEM((hd, depth), BF),
        ),
        in_specs=[anywhere] * 9,
        out_specs=(vmem,) * 5,
        scratch_shapes=[
            pltpu.VMEM((4, tv, depth), BF),
            pltpu.VMEM((depth, hd), BF),
            pltpu.VMEM((hd, depth), BF),
            pltpu.VMEM((HEADS, 3, tv, HS), BF),
            pltpu.VMEM((HEADS, 3, ta, HS), BF),
            pltpu.VMEM((2 * n_chip, 3, tv, HS), BF),
            pltpu.VMEM((n_pair, 2, 2, 3, ta, HS), BF),
            pltpu.VMEM((n_pair, 2, n_tile, rows, wide), kept),
            pltpu.VMEM((n_pair, 2, n_tile, rows, wide), kept),
            pltpu.VMEM((2, rows, lanes), F32),
            pltpu.VMEM((2, lanes, rows), F32),
            pltpu.VMEM((3, n_pair, 2, n_tile, 8, wide), F32),
            pltpu.VMEM((2, rounded_up(3 * n_chip // 2, 8), rows), F32),
            pltpu.VMEM((2, n_chip, rounded_up(3 * n_chip // 2, 8), rows), F32),
            pltpu.VMEM((n_pair, 8, wide), F32),
            pltpu.VMEM((n_pair, 2, n_pair, 8, wide), F32),
            pltpu.VMEM((2, rows, lanes), F32),
            pltpu.VMEM((3, n_pair, 2, 1, wide), F32),
            pltpu.VMEM((n_tile, rows, WIDE), F32),
            pltpu.VMEM((2 * n_pair, WIDE, wide), F32),
            pltpu.VMEM((2 * n_chip, tv, WIDE), BF),
            pltpu.VMEM((2 * n_chip, tv, WIDE), BF),
            pltpu.VMEM((2, tv, WIDE), BF),
            pltpu.VMEM((n_pair, 2, 2, WIDE, ta), BF),
            pltpu.VMEM((n_pair, 2, WIDE, ta), BF),
            pltpu.VMEM((n_pair, 2, WIDE, ta), BF),
            pltpu.VMEM((n_pair, 2, WIDE, ta), BF),
            pltpu.VMEM((HEADS, ta, WIDE), BF),
            dma((9,)),
        ]
        + [dma(shape) for shape in remote for _ in range(2)],
        compiler_params=pltpu.CompilerParams(
            collective_id=0, has_side_effects=True, vmem_limit_bytes=50 * 1024 * 1024
        ),
    )(*(pltpu.with_memory_space_constraint(array, pltpu.HBM) for array in arrays))
    return pl.pallas_call(
        output_kernel,
        out_shape=(video_out, audio_out, video_out, audio_out),
        in_specs=[vmem] * 5,
        out_specs=(anywhere,) * 4,
        scratch_shapes=[
            pltpu.VMEM((2, tv, depth), BF),
            dma((2,)),
            dma((2, 3)),
        ],
        compiler_params=pltpu.CompilerParams(vmem_limit_bytes=16 * 1024 * 1024),
    )(*held)


def solution(mesh):
    rows_v, rows_a = P(("vid", "aud"), None), P(("aud", "vid"), None)
    return jax.shard_map(
        functools.partial(on_device, mesh.shape["vid"], mesh.shape["aud"]),
        mesh=mesh,
        in_specs=(rows_v, rows_a, P(), P(), P(), P(), P(), rows_v, rows_a),
        out_specs=(rows_v, rows_a, rows_v, rows_a),
        check_vma=False,
    )
```
